256 devices in a mesh: lon: 64 (over x_lo, y, z), lat: 4 (over x_hi, core).
Axes of the slice: x: 4 (x_hi: 2, x_lo: 2; x = x_hi * 2 + x_lo), y: 4, z: 8, core: 2. Of those that a mesh axis runs over, the one named last changes fastest.
Arguments:
- hidden_in: bfloat16 [8, 128, 1024, 512], P(None, None, 'lon', 'lat'), may hold values from -6 to 6
- w_conv1: bfloat16 [3, 3, 128, 128], replicated, may hold values from -0.1875 to 0.1875
- b_conv1: float32 [128], replicated, may hold values from -3 to 3
- w_conv2: bfloat16 [3, 3, 128, 12], replicated, may hold values from -0.1875 to 0.1875
- b_conv2: float32 [12], replicated, may hold values from -3.5 to 3.5
- state: float32 [6, 8, 1024, 512], P(None, None, 'lon', 'lat'), may hold values from -6 to 6
Outputs:
- velocity: float32 [12, 8, 1024, 512], P(None, None, 'lon', 'lat')
- tendency: float32 [6, 8, 1024, 512], P(None, None, 'lon', 'lat')
The draws below stay inside these ranges and needn't reach their ends.
All inputs are finite; a program needn't handle non-finite values.
Results may differ from the reference program's by a relative error of at most 0.0013.
Values may be sent and summed in bfloat16 or wider, within the bound.
A program may use at most 128 MiB of HBM per device.

```python
import math
import jax
import jax.numpy as jnp
from jax import lax

CH = 128
VARS = 6
VEL = 12
LEV = 8
NLON = 1024
NLAT = 512


def draw_b_conv2(key, part):
    flip_key = jax.random.fold_in(key, 11)
    drift_key = jax.random.fold_in(key, 12)
    zonal_key = jax.random.fold_in(key, 13)
    flip_bits = jax.random.randint(flip_key, (VEL,), 0, 2)
    drift_bias = (2.0 * flip_bits.astype(jnp.float32) - 1.0) * jax.random.uniform(drift_key, (VEL,), jnp.float32, 2.5, 3.5)
    zonal_bias = 0.5 * jax.random.truncated_normal(zonal_key, -3.0, 3.0, (VEL,), jnp.float32)
    north_mask = lax.broadcasted_iota(jnp.int32, (VEL,), 0) % 2
    return jnp.where(north_mask == 1, drift_bias, zonal_bias)


def draw_state(key, part):
    shape_full = (VARS, LEV, NLON, NLAT)
    lon_pos = lax.broadcasted_iota(jnp.int32, shape_full, 2)
    lat_pos = lax.broadcasted_iota(jnp.int32, shape_full, 3)
    parity = (lon_pos + lat_pos) % 2
    alt_sign = 1.0 - 2.0 * parity.astype(jnp.float32)
    size_term = jax.random.uniform(key, shape_full, jnp.float32, 1.5, 5.5)
    return alt_sign * size_term


def level_of(key, extent, split, low, largest):
    gain, own = 1.0, jax.random.fold_in(key, 6)
    for axis_at, parts in split:
        draws = jnp.exp(jax.random.uniform(jax.random.fold_in(own, axis_at), (parts,), jnp.float32, low / len(split), largest / len(split)))
        gain = gain * jnp.repeat(draws, extent[axis_at] // parts).reshape([-1 if axis == axis_at else 1 for axis in range(len(extent))])
    return gain


def normal_values(key, dims, scale, reach, pieces=(), kind=jnp.bfloat16):
    result = jax.random.normal(key, dims, jnp.float32) * scale
    if len(pieces) > 0:
        result = level_of(key, dims, pieces, -0.22, 0.18) * result
    return jnp.clip(result, min=-reach, max=reach).astype(kind)


def setup_inputs(seed: int = 0) -> dict:
    seeds = jax.random.split(jax.random.key(seed), 7)
    hidden_in = normal_values(seeds[0], (LEV, CH, NLON, NLAT), 1.0, 6.0, ((2, 64), (3, 4)))
    w_conv1 = normal_values(seeds[1], (3, 3, CH, CH), (9 * CH) ** -0.5, 0.1875)
    b_conv1 = normal_values(seeds[2], (CH,), 0.5, 3.0, (), jnp.float32)
    w_conv2 = normal_values(seeds[3], (3, 3, CH, VEL), (9 * CH) ** -0.5, 0.1875)
    b_conv2 = draw_b_conv2(jax.random.fold_in(seeds[6], 71), 0)
    state = draw_state(jax.random.fold_in(seeds[6], 71), 0)
    return {"hidden_in": hidden_in, "w_conv1": w_conv1, "b_conv1": b_conv1, "w_conv2": w_conv2, "b_conv2": b_conv2, "state": state}


time_step = 0.5
speed_cap = 0.6
cos_floor = 0.5


def wrap_pad(field, width):
    field = jnp.concatenate([field[..., -width:, :], field, field[..., :width, :]], axis=-2)
    widths = [(0, 0)] * (field.ndim - 1) + [(width, width)]
    return jnp.pad(field, widths)


def conv_level(padded, weight):
    out_x = padded.shape[1] - 2
    out_y = padded.shape[2] - 2
    total = jnp.zeros((weight.shape[3], out_x, out_y), jnp.float32)
    for row_off in range(3):
        for col_off in range(3):
            window = padded[:, row_off:row_off + out_x, col_off:col_off + out_y].astype(jnp.float32)
            total = total + jnp.einsum("cxy,co->oxy", window, weight[row_off, col_off].astype(jnp.float32))
    return total


def reference(hidden_in, w_conv1, b_conv1, w_conv2, b_conv2, state):
    def level(features):
        first = conv_level(wrap_pad(features, 1), w_conv1) + b_conv1[:, None, None]
        hidden = jax.nn.silu(first).astype(jnp.bfloat16)
        second = conv_level(wrap_pad(hidden, 1), w_conv2) + b_conv2[:, None, None]
        return speed_cap * jnp.tanh(second)

    velocity = jnp.transpose(lax.map(level, hidden_in), (1, 0, 2, 3))
    n_lat = state.shape[3]
    rows = jnp.arange(n_lat).astype(jnp.float32)
    latitude = (rows + 0.5) * (math.pi / n_lat) - 0.5 * math.pi
    cosine = jnp.maximum(jnp.cos(latitude), cos_floor)
    metric = 1.0 / cosine
    zonal = velocity[0::2]
    north = velocity[1::2]
    zonal_pad = wrap_pad(zonal, 1)
    flux_pad = wrap_pad(north * cosine, 1)
    divergence = metric * ((zonal_pad[..., 2:, 1:-1] - zonal_pad[..., :-2, 1:-1]) * 0.5
                           + (flux_pad[..., 1:-1, 2:] - flux_pad[..., 1:-1, :-2]) * 0.5)

    def rate(field):
        padded = wrap_pad(field, 1)
        centre = padded[..., 1:-1, 1:-1]
        back_x = centre - padded[..., :-2, 1:-1]
        fore_x = padded[..., 2:, 1:-1] - centre
        back_y = centre - padded[..., 1:-1, :-2]
        fore_y = padded[..., 1:-1, 2:] - centre
        advect = metric * (jnp.maximum(zonal, 0.0) * back_x + jnp.minimum(zonal, 0.0) * fore_x) \
            + jnp.maximum(north, 0.0) * back_y + jnp.minimum(north, 0.0) * fore_y
        return -(advect + centre * divergence)

    rate_one = rate(state)
    rate_two = rate(state + 0.5 * time_step * rate_one)
    rate_three = rate(state + 0.5 * time_step * rate_two)
    rate_four = rate(state + time_step * rate_three)
    tendency = (rate_one + 2.0 * rate_two + 2.0 * rate_three + rate_four) / 6.0
    return velocity, tendency
```

```python
import functools
import math

import jax
import jax.numpy as jnp
import numpy as np
from jax import lax
from jax.experimental import pallas as pl
from jax.experimental.pallas import tpu as pltpu
from jax.sharding import PartitionSpec as P

MESH = pl.DeviceIdType.MESH
F32 = jnp.float32
BF16 = jnp.bfloat16
TIME_STEP = 0.5
SPEED_CAP = 0.6
COS_FLOOR = 0.5
NV = 6
NC = 12
NF = 18
LV = 8
NX = 16
NY = 128
CH = 128
M = 4
EX = NX + 2 * M
NR = NX + 2


def lat_tables(n_lat_dev):
    n_lat = n_lat_dev * NY
    out = np.zeros((n_lat_dev, 2, LV, 2 * NY), np.float32)
    for d in range(n_lat_dev):
        lane = np.arange(2 * NY)
        y = np.where(lane < NY + NY // 2, lane, lane - 2 * NY) + d * NY
        phi = (y + 0.5) * (math.pi / n_lat) - 0.5 * math.pi
        inside = ((y >= 0) & (y < n_lat)).astype(np.float32)
        out[d, 0] = np.maximum(np.cos(phi), COS_FLOOR)[None]
        out[d, 1] = (SPEED_CAP * inside)[None]
    return out


def lanes(shape):
    return lax.broadcasted_iota(jnp.int32, shape, len(shape) - 1)


def roll(v, s):
    s = s % NY
    return v if s == 0 else pltpu.roll(v, s, v.ndim - 1)


def kernel(n_lon, n_lat, x_hbm, w1_ref, b1_ref, w2_ref, b2_ref, st_ref, tab_ref,
           vel_ref, tend_ref,
           xin, xt, ht, lhs1, lhs2, oh, ohe, bias, xe, xh, xc, pm, pe, fm, fe, pk, pr, rowr, epk, epr,
           in_sem, ls, lr, ns, nr, ps, prs, rs, rr, qls, qlr, qs, qr):
    lon = lax.axis_index("lon")
    lat = lax.axis_index("lat")
    left = (lax.rem(lon + n_lon - 1, n_lon), lat)
    right = (lax.rem(lon + 1, n_lon), lat)
    south = (lon, lat - 1)
    north = (lon, lat + 1)
    has_s = lat > 0
    has_n = lat < n_lat - 1

    xh[...] = jnp.zeros_like(xh)
    pr[...] = jnp.zeros_like(pr)

    barrier = pltpu.get_barrier_semaphore()
    for dev in (left, right):
        pl.semaphore_signal(barrier, inc=1, device_id=dev, device_id_type=MESH)

    @pl.when(has_s)
    def _():
        pl.semaphore_signal(barrier, inc=1, device_id=south, device_id_type=MESH)

    @pl.when(has_n)
    def _():
        pl.semaphore_signal(barrier, inc=1, device_id=north, device_id_type=MESH)

    loads = [pltpu.make_async_copy(x_hbm.at[l], xin.at[l], in_sem.at[l]) for l in range(LV)]
    for c in loads:
        c.start()

    for b in range(3):
        for a in range(3):
            lhs1[0, b * CH:(b + 1) * CH, a * CH:(a + 1) * CH] = jnp.transpose(w1_ref[a, b], (1, 0))
    for lp in range(1, LV // 2):
        lhs1[lp, :, 0:3 * CH] = lhs1[0, :, 0:3 * CH]
    lhs2[...] = jnp.zeros_like(lhs2)
    for b in range(3):
        for off in range(4):
            for r in range(2):
                a = r - off + 2
                if 0 <= a <= 2:
                    base = b * 64 + off * 16
                    lhs2[base:base + NC, r * CH:(r + 1) * CH] = w2_ref[a, b]
    bias[...] = jnp.transpose(jnp.broadcast_to(b1_ref[...], (CH, CH)), (1, 0))
    k_id = lax.broadcasted_iota(jnp.int32, (CH, 2 * NY), 0)
    lane2 = lanes((CH, 2 * NY))
    half = (k_id // 16) % 2
    target = half * NY + jnp.where(k_id < 64, 0, NY - 1)
    hit = lane2 == target

    @pl.loop(0, NX)
    def _(x):
        oh[x] = jnp.where(hit & (k_id % 16 == x), 1.0, 0.0).astype(BF16)
        want_hi = (k_id == NY - 1) & (lane2 == x)
        want_lo = (k_id == 0) & (lane2 == NY + x)
        ohe[x] = jnp.where(want_hi | want_lo, 1.0, 0.0).astype(BF16)

    zero_rows = jnp.zeros((NF, M, LV, NY), F32)
    fe[:, 0:M] = zero_rows
    fe[:, M + NX:EX] = zero_rows
    fm[0:NC, 0:M] = zero_rows[:NC]
    fm[0:NC, M + NX:EX] = zero_rows[:NC]
    for v in range(NV):
        fm[NC + v, M:M + NX] = jnp.transpose(st_ref[v], (1, 0, 2))

    hi = jnp.zeros((CH, NY), F32)
    lo = jnp.zeros((CH, NY), F32)
    for l in range(LV):
        loads[l].wait()
        xt[l, 1:NX + 1] = jnp.transpose(xin[l], (1, 0, 2))
        row = jnp.concatenate([xt[l, 1 + x] for x in range(NX)], axis=1)
        res = jnp.dot(row, ohe[...].reshape(NX * NY, 2 * NY), preferred_element_type=F32)
        hi = hi + roll(res[:, :NY], 16 * l)
        lo = lo + roll(res[:, NY:], 16 * l)
    xe[0] = hi.astype(BF16)
    xe[1] = lo.astype(BF16)

    pl.semaphore_wait(barrier, 2 + has_s.astype(jnp.int32) + has_n.astype(jnp.int32))

    def rcopy(src, dst, ss, rs_, dev):
        return pltpu.make_async_remote_copy(src_ref=src, dst_ref=dst, send_sem=ss, recv_sem=rs_,
                                            device_id=dev, device_id_type=MESH)

    def lat_exchange(src_n, src_s, dst_from_s, dst_from_n, sems, semr):
        to_n = rcopy(src_n, dst_from_s, sems.at[0], semr.at[0], north)
        to_s = rcopy(src_s, dst_from_n, sems.at[1], semr.at[1], south)

        @pl.when(has_n)
        def _():
            to_n.start()

        @pl.when(has_s)
        def _():
            to_s.start()

        def finish():
            @pl.when(has_s)
            def _():
                to_n.wait_recv()
                to_s.wait_send()

            @pl.when(has_n)
            def _():
                to_s.wait_recv()
                to_n.wait_send()
        return finish

    lane8 = lanes((LV, NY))

    def pack_lat(f, get_m, get_e):
        to_n = jnp.zeros((LV, NY), F32)
        to_s = jnp.zeros((LV, NY), F32)
        for r in range(NR):
            m = get_m(r)
            e = get_e(r)
            mine = (lane8 >= 5 * r) & (lane8 < 5 * r + 5)
            to_n = jnp.where(mine, roll(jnp.where(lane8 == 0, e, m), 5 * r + 4), to_n)
            to_s = jnp.where(mine, roll(jnp.where(lane8 == NY - 1, e, m), 5 * r + 1), to_s)
        pk[0, f] = to_n
        pk[1, f] = to_s

    def add_lat(f, get_m, get_e):
        edges = []
        for r in range(NR):
            a = roll(pr[0, f], -(5 * r + 4))
            b = roll(pr[1, f], -(5 * r + 1))
            if get_m is not None:
                fm[f, M - 1 + r] = get_m(r) + jnp.where(lane8 == 0, a, 0.0) + jnp.where(lane8 == NY - 1, b, 0.0)
            edge = get_e(r) + jnp.where(lane8 >= NY - 4, a, 0.0) + jnp.where(lane8 < 4, b, 0.0)
            fe[f, M - 1 + r] = edge
            edges.append(edge)
        for side in range(2):
            acc = jnp.zeros((LV, NY), F32)
            for r in range(5):
                src = edges[r if side == 0 else NR - 5 + r]
                acc = jnp.where((lane8 >= 8 * r) & (lane8 < 8 * r + 8), roll(src, 8 * r + 4), acc)
            epk[side, f] = acc

    def add_edge_rows(f):
        for side in range(2):
            for r in range(5):
                x = (r if side == 0 else M + NX - 1 + r)
                t = roll(epr[side, f], -(8 * r + 4))
                fe[f, x] = fe[f, x] + jnp.where((lane8 < 4) | (lane8 >= NY - 4), t, 0.0)

    x_lat = lat_exchange(xe.at[0], xe.at[1], xh.at[0], xh.at[1], ls, lr)
    x_left = rcopy(xt.at[:, 1], xt.at[:, NX + 1], ns.at[0], nr.at[0], left)
    x_right = rcopy(xt.at[:, NX], xt.at[:, 0], ns.at[1], nr.at[1], right)
    x_left.start()
    x_right.start()
    x_lat()
    c_left = rcopy(xh, xc.at[1], ns.at[2], nr.at[2], left)
    c_right = rcopy(xh, xc.at[0], ns.at[3], nr.at[3], right)
    c_left.start()
    c_right.start()
    c_left.wait()
    c_right.wait()

    xpos = lanes((CH, NY)) % NX
    kinds = []
    for side in range(2):
        b = 2 * side
        own = xh[side].astype(F32)
        from_l = xc[0, side].astype(F32)
        from_r = xc[1, side].astype(F32)
        t0 = jnp.where(xpos == 0, roll(from_l, -(NX - 1)), roll(own, 1)).astype(BF16)
        t2 = jnp.where(xpos == NX - 1, roll(from_r, NX - 1), roll(own, -1)).astype(BF16)
        taps = jnp.concatenate([t0, xh[side], t2], axis=0)
        e = jnp.dot(lhs1[0, b * CH:(b + 1) * CH, 0:3 * CH], taps, preferred_element_type=F32)
        e_hi = e.astype(BF16).astype(F32)
        kinds += [e_hi, e - e_hi]
    group = lanes((CH, NY)) // 32
    for lp in range(LV // 2):
        inj = jnp.zeros((CH, NY), F32)
        for kind in range(4):
            inj = jnp.where(group == kind, roll(kinds[kind], 32 * kind - 32 * lp), inj)
        zero = jnp.zeros((CH, NY), BF16)
        lhs1[lp, 0:CH, 3 * CH:] = zero
        lhs1[lp, CH:2 * CH, 3 * CH:] = inj.astype(BF16)
        lhs1[lp, 2 * CH:, 3 * CH:] = zero

    zero8 = jnp.zeros((LV, NY), F32)

    @pl.loop(NC, NF)
    def _(f):
        pack_lat(f, lambda r: fm[f, M - 1 + r] if 0 < r < NR - 1 else zero8, lambda r: zero8)

    q_left = rcopy(fm.at[NC:NF, M:M + 4], fm.at[NC:NF, M + NX:M + NX + 4], qs.at[0], qr.at[0], left)
    q_right = rcopy(fm.at[NC:NF, M + NX - 4:M + NX], fm.at[NC:NF, 0:4], qs.at[1], qr.at[1], right)
    q_left.start()
    q_right.start()
    q_lat = lat_exchange(pk.at[0, NC:NF], pk.at[1, NC:NF], pr.at[0, NC:NF], pr.at[1, NC:NF], qls, qlr)
    q_lat()

    @pl.loop(NC, NF)
    def _(f):
        add_lat(f, None, lambda r: zero8)

    qe_left = rcopy(epk.at[0, NC:NF], epr.at[1, NC:NF], qs.at[2], qr.at[2], left)
    qe_right = rcopy(epk.at[1, NC:NF], epr.at[0, NC:NF], qs.at[3], qr.at[3], right)
    qe_left.start()
    qe_right.start()
    q_copies = [q_left, q_right, qe_left, qe_right]

    x_left.wait()
    x_right.wait()

    lane1 = lanes((CH, NY))

    @pl.loop(0, LV // 2)
    def _(lp):
        @pl.loop(0, NX)
        def _(x):
            rhs = jnp.concatenate(
                [xt[2 * lp + h, pl.ds(x, 3)].reshape(3 * CH, NY) for h in range(2)], axis=1)
            rhs = jnp.concatenate([rhs, oh[x]], axis=0)
            s = jnp.dot(lhs1[lp], rhs, preferred_element_type=F32)
            for h in range(2):
                c = slice(h * NY, (h + 1) * NY)
                pre = s[CH:2 * CH, c] + bias[...]
                pre = pre + jnp.where(lane1 == 0, 0.0, roll(s[0:CH, c], 1))
                pre = pre + jnp.where(lane1 == NY - 1, 0.0, roll(s[2 * CH:, c], -1))
                half_pre = 0.5 * pre
                ht[2 * lp + h, x] = (half_pre + half_pre * jnp.tanh(half_pre)).astype(BF16)

    lane64 = lanes((64, NY))

    @pl.loop(0, LV // 2)
    def _(lp):
        prev = [None, None]
        for p in range(NX // 2):
            rhs = jnp.concatenate(
                [ht[2 * lp + h, 2 * p:2 * p + 2].reshape(2 * CH, NY) for h in range(2)], axis=1)
            s = jnp.dot(lhs2[...], rhs, preferred_element_type=F32)
            for h in range(2):
                c = slice(h * NY, (h + 1) * NY)
                up = roll(s[0:64, c], 1)
                dn = roll(s[128:192, c], -1)
                main = s[64:128, c] + jnp.where(lane64 == 0, 0.0, up) + jnp.where(lane64 == NY - 1, 0.0, dn)
                edge = jnp.where(lane64 == 0, up, 0.0) + jnp.where(lane64 == NY - 1, dn, 0.0)
                now = (main, edge)
                l = 2 * lp + h
                rows = [(2 * p - 1, 0), (2 * p, 1)]
                if p == NX // 2 - 1:
                    rows += [(2 * p + 1, 2), (2 * p + 2, 3)]
                for xo, off in rows:
                    for ref, val, old in zip((pm, pe), now, prev[h] or (None, None)):
                        t = val[off * 16:off * 16 + NC]
                        if off < 2 and old is not None:
                            t = t + old[(off + 2) * 16:(off + 2) * 16 + NC]
                        ref[pl.ds((xo + 1) * LV + l, NC, stride=NR * LV), :] = t
                prev[h] = now

    @pl.loop(0, NC)
    def _(f):
        pack_lat(f, lambda r: pm[pl.ds((f * NR + r) * LV, LV), :], lambda r: pe[pl.ds((f * NR + r) * LV, LV), :])

    lat_exchange(pk.at[0, 0:NC], pk.at[1, 0:NC], pr.at[0, 0:NC], pr.at[1, 0:NC], ps, prs)()

    @pl.loop(0, NC)
    def _(f):
        add_lat(f, lambda r: pm[pl.ds((f * NR + r) * LV, LV), :], lambda r: pe[pl.ds((f * NR + r) * LV, LV), :])

    r_left = rcopy(fm.at[0:NC, M - 1:M + 4], rowr.at[1], rs.at[0], rr.at[0], left)
    r_right = rcopy(fm.at[0:NC, M + NX - 4:M + NX + 1], rowr.at[0], rs.at[1], rr.at[1], right)
    e_left = rcopy(epk.at[0, 0:NC], epr.at[1, 0:NC], rs.at[2], rr.at[2], left)
    e_right = rcopy(epk.at[1, 0:NC], epr.at[0, 0:NC], rs.at[3], rr.at[3], right)
    for c in (e_left, e_right, r_left, r_right):
        c.start()
    for c in (e_left, e_right, r_left, r_right):
        c.wait()

    @pl.loop(0, NC)
    def _(f):
        for side in range(2):
            for r in range(5):
                x = (r if side == 0 else M + NX - 1 + r)
                fm[f, x] = fm[f, x] + rowr[side, f, r]
        add_edge_rows(f)

    for c in q_copies:
        c.wait()

    @pl.loop(NC, NF)
    def _(f):
        add_edge_rows(f)

    cos_m = tab_ref[lat, 0, :, 0:NY]
    cos_e = tab_ref[lat, 0, :, NY:]
    cap_m = tab_ref[lat, 1, :, 0:NY]
    cap_e = tab_ref[lat, 1, :, NY:]
    met_m = 1.0 / cos_m
    met_e = 1.0 / cos_e

    def shift(m, e, step):
        sh = 1 if step < 0 else -1
        edge = 0 if step < 0 else NY - 1
        rm, re = roll(m, sh), roll(e, sh)
        at = lanes(m.shape) == edge
        return jnp.where(at, re, rm), jnp.where(at, rm, re)

    @pl.loop(0, NV)
    def _(v):
        bu = b2_ref[2 * v]
        bv = b2_ref[2 * v + 1]
        um = cap_m * jnp.tanh(fm[2 * v] + bu)
        ue = cap_e * jnp.tanh(fe[2 * v] + bu)
        vm = cap_m * jnp.tanh(fm[2 * v + 1] + bv)
        ve = cap_e * jnp.tanh(fe[2 * v + 1] + bv)
        vel_ref[2 * v] = jnp.transpose(um[M:M + NX], (1, 0, 2))
        vel_ref[2 * v + 1] = jnp.transpose(vm[M:M + NX], (1, 0, 2))
        i = slice(1, EX - 1)
        fn_m, fn_e = shift(vm[i] * cos_m, ve[i] * cos_e, 1)
        fs_m, fs_e = shift(vm[i] * cos_m, ve[i] * cos_e, -1)

        def coef(u, vv, met, fn, fs):
            div = met * ((u[2:] - u[:-2]) * 0.5 + (fn - fs) * 0.5)
            up, un = met * jnp.maximum(u[i], 0.0), met * jnp.minimum(u[i], 0.0)
            vp, vn = jnp.maximum(vv[i], 0.0), jnp.minimum(vv[i], 0.0)
            return (un - up) + (vn - vp) - div, up, un, vp, vn

        cm = coef(um, vm, met_m, fn_m, fs_m)
        ce = coef(ue, ve, met_e, fn_e, fs_e)

        def rate(qm, qe, k):
            n = EX - 2 * k
            nm, ne = shift(qm[1:-1], qe[1:-1], 1)
            sm, se = shift(qm[1:-1], qe[1:-1], -1)

            def one(q, c, qn, qs):
                c0, up, un, vp, vn = (t[k - 1:k - 1 + n] for t in c)
                return c0 * q[1:-1] + up * q[:-2] - un * q[2:] + vp * qs - vn * qn
            return one(qm, cm, nm, sm), one(qe, ce, ne, se)

        qm = fm[NC + v]
        qe = fe[NC + v]
        r1m, r1e = rate(qm, qe, 1)
        tot = r1m[3:3 + NX]
        r2m, r2e = rate(qm[1:-1] + 0.25 * r1m, qe[1:-1] + 0.25 * r1e, 2)
        tot = tot + 2.0 * r2m[2:2 + NX]
        r3m, r3e = rate(qm[2:-2] + 0.25 * r2m, qe[2:-2] + 0.25 * r2e, 3)
        tot = tot + 2.0 * r3m[1:1 + NX]
        r4m, _ = rate(qm[3:-3] + 0.5 * r3m, qe[3:-3] + 0.5 * r3e, 4)
        tend_ref[v] = jnp.transpose((tot + r4m) * (1.0 / 6.0), (1, 0, 2))


def solution(mesh):
    n_lon, n_lat = mesh.shape["lon"], mesh.shape["lat"]
    tables = lat_tables(n_lat)

    def body(hidden_in, w1, b1, w2, b2, state):
        vmem = pl.BlockSpec(memory_space=pltpu.VMEM)
        dma = pltpu.SemaphoreType.DMA
        return pl.pallas_call(
            functools.partial(kernel, n_lon, n_lat),
            out_shape=(jax.ShapeDtypeStruct((NC, LV, NX, NY), F32),
                       jax.ShapeDtypeStruct((NV, LV, NX, NY), F32)),
            in_specs=[pl.BlockSpec(memory_space=pl.ANY), vmem, vmem, vmem,
                      pl.BlockSpec(memory_space=pltpu.SMEM), vmem, vmem],
            out_specs=(vmem, vmem),
            scratch_shapes=[
                pltpu.VMEM((LV, CH, NX, NY), BF16),
                pltpu.VMEM((LV, NX + 2, CH, NY), BF16),
                pltpu.VMEM((LV, NX, CH, NY), BF16),
                pltpu.VMEM((LV // 2, 3 * CH, 4 * CH), BF16),
                pltpu.VMEM((192, 2 * CH), BF16),
                pltpu.VMEM((NX, CH, 2 * NY), BF16),
                pltpu.VMEM((NX, CH, 2 * NY), BF16),
                pltpu.VMEM((CH, NY), F32),
                pltpu.VMEM((2, CH, NY), BF16),
                pltpu.VMEM((2, CH, NY), BF16),
                pltpu.VMEM((2, 2, CH, NY), BF16),
                pltpu.VMEM((NC * NR * LV, NY), F32),
                pltpu.VMEM((NC * NR * LV, NY), F32),
                pltpu.VMEM((NF, EX, LV, NY), F32),
                pltpu.VMEM((NF, EX, LV, NY), F32),
                pltpu.VMEM((2, NF, LV, NY), F32),
                pltpu.VMEM((2, NF, LV, NY), F32),
                pltpu.VMEM((2, NC, 5, LV, NY), F32),
                pltpu.VMEM((2, NF, LV, NY), F32),
                pltpu.VMEM((2, NF, LV, NY), F32),
                dma((LV,)), dma((2,)), dma((2,)), dma((4,)), dma((4,)),
                dma((2,)), dma((2,)), dma((4,)), dma((4,)),
                dma((2,)), dma((2,)), dma((4,)), dma((4,)),
            ],
            compiler_params=pltpu.CompilerParams(
                collective_id=0, has_side_effects=True, vmem_limit_bytes=60 * 1024 * 1024),
        )(hidden_in, w1, b1.reshape(1, CH), jnp.transpose(w2, (0, 1, 3, 2)), b2, state,
          jnp.asarray(tables))

    spread = P(None, None, "lon", "lat")
    return jax.shard_map(
        body, mesh=mesh, in_specs=(spread, P(), P(), P(), P(), spread),
        out_specs=(spread, spread), check_vma=False)
```

```python
import functools
import math

import jax
import jax.numpy as jnp
import numpy as np
from jax import lax
from jax.experimental import pallas as pl
from jax.experimental.pallas import tpu as pltpu
from jax.sharding import PartitionSpec as P

MESH = pl.DeviceIdType.MESH
F32 = jnp.float32
BF16 = jnp.bfloat16
TIME_STEP = 0.5
SPEED_CAP = 0.6
COS_FLOOR = 0.5
NV = 6
NC = 12
NF = 18
LV = 8
NX = 16
NY = 128
CH = 128
M = 4
EX = NX + 2 * M
NR = NX + 2
NP = 2 * NC + NV
HALF = LV // 2


def lat_tables(n_lat_dev):
    n_lat = n_lat_dev * NY
    out = np.zeros((n_lat_dev, 2, LV, 2 * NY), np.float32)
    for d in range(n_lat_dev):
        lane = np.arange(2 * NY)
        y = np.where(lane < NY + NY // 2, lane, lane - 2 * NY) + d * NY
        phi = (y + 0.5) * (math.pi / n_lat) - 0.5 * math.pi
        inside = ((y >= 0) & (y < n_lat)).astype(np.float32)
        out[d, 0] = np.maximum(np.cos(phi), COS_FLOOR)[None]
        out[d, 1] = (SPEED_CAP * inside)[None]
    return out


def lanes(shape):
    return lax.broadcasted_iota(jnp.int32, shape, len(shape) - 1)


def roll(v, s):
    s = s % NY
    return v if s == 0 else pltpu.roll(v, s, v.ndim - 1)


def kernel(n_lon, n_lat, x_hbm, w1_ref, b1_ref, w2_ref, b2_ref, st_ref, tab_ref,
           vel_ref, tend_ref,
           xin, xt, ht, lhs1, lhs2, oh, ohe, bias, xe, xh, xc, pm, pe, fm, fe, pk, pr, rowr, epk, epr,
           in_sem, x_s, x_r, row_s, row_r, cor_s, cor_r, lat_s, lat_r, lon_s, lon_r, q_s, q_r):
    lon = lax.axis_index("lon")
    lat = lax.axis_index("lat")
    left = (lax.rem(lon + n_lon - 1, n_lon), lat)
    right = (lax.rem(lon + 1, n_lon), lat)
    south = (lon, lat - 1)
    north = (lon, lat + 1)
    has_s = lat > 0
    has_n = lat < n_lat - 1

    for side, has in ((0, has_s), (1, has_n)):
        @pl.when(jnp.logical_not(has))
        def _():
            xh[side] = jnp.zeros((CH, NY), BF16)
            pr[side] = jnp.zeros((NP, LV, NY), F32)

    barrier = pltpu.get_barrier_semaphore()
    for dev in (left, right):
        pl.semaphore_signal(barrier, inc=1, device_id=dev, device_id_type=MESH)

    @pl.when(has_s)
    def _():
        pl.semaphore_signal(barrier, inc=1, device_id=south, device_id_type=MESH)

    @pl.when(has_n)
    def _():
        pl.semaphore_signal(barrier, inc=1, device_id=north, device_id_type=MESH)

    loads = [pltpu.make_async_copy(x_hbm.at[l], xin.at[l], in_sem.at[l]) for l in range(LV)]
    for c in loads:
        c.start()

    for b in range(3):
        for a in range(3):
            lhs1[0, b * CH:(b + 1) * CH, a * CH:(a + 1) * CH] = jnp.transpose(w1_ref[a, b], (1, 0))
    for lp in range(1, LV // 2):
        lhs1[lp, :, 0:3 * CH] = lhs1[0, :, 0:3 * CH]
    lhs2[...] = jnp.zeros_like(lhs2)
    for b in range(3):
        for off in range(4):
            for r in range(2):
                a = r - off + 2
                if 0 <= a <= 2:
                    base = b * 64 + off * 16
                    lhs2[base:base + NC, r * CH:(r + 1) * CH] = w2_ref[a, b]
    bias[...] = jnp.transpose(jnp.broadcast_to(b1_ref[...], (CH, CH)), (1, 0))
    k_id = lax.broadcasted_iota(jnp.int32, (CH, 2 * NY), 0)
    lane2 = lanes((CH, 2 * NY))
    half = (k_id // 16) % 2
    target = half * NY + jnp.where(k_id < 64, 0, NY - 1)
    hit = lane2 == target

    @pl.loop(0, NX)
    def _(x):
        oh[x] = jnp.where(hit & (k_id % 16 == x), 1.0, 0.0).astype(BF16)
        want_hi = (k_id == NY - 1) & (lane2 == x)
        want_lo = (k_id == 0) & (lane2 == NY + x)
        ohe[x] = jnp.where(want_hi | want_lo, 1.0, 0.0).astype(BF16)

    ht[:, 0] = jnp.zeros((LV, CH, NY), BF16)
    ht[:, NX + 1] = jnp.zeros((LV, CH, NY), BF16)

    def rcopy(src, dst, ss, rs_, dev):
        return pltpu.make_async_remote_copy(src_ref=src, dst_ref=dst, send_sem=ss, recv_sem=rs_,
                                            device_id=dev, device_id_type=MESH)

    hi = jnp.zeros((CH, NY), F32)
    lo = jnp.zeros((CH, NY), F32)
    rows_left, rows_right = [], []
    for l in range(LV):
        loads[l].wait()
        xt[l, 1:NX + 1] = jnp.transpose(xin[l], (1, 0, 2))
        row = jnp.concatenate([xt[l, 1 + x] for x in range(NX)], axis=1)
        res = jnp.dot(row, ohe[...].reshape(NX * NY, 2 * NY), preferred_element_type=F32)
        hi = hi + roll(res[:, :NY], 16 * l)
        lo = lo + roll(res[:, NY:], 16 * l)
        if l == HALF - 1:
            pl.semaphore_wait(barrier, 2 + has_s.astype(jnp.int32) + has_n.astype(jnp.int32))
        if (l + 1) % HALF == 0:
            g = l // HALF
            part = slice(g * HALF, (g + 1) * HALF)
            rows_left.append(rcopy(xt.at[part, 1], xt.at[part, NX + 1], row_s.at[g], row_r.at[g], left))
            rows_right.append(rcopy(xt.at[part, NX], xt.at[part, 0], row_s.at[2 + g], row_r.at[2 + g], right))
            rows_left[-1].start()
            rows_right[-1].start()
    xe[0] = hi.astype(BF16)
    xe[1] = lo.astype(BF16)

    def lat_exchange(src_n, src_s, dst_from_s, dst_from_n, sems, semr, at):
        to_n = rcopy(src_n, dst_from_s, sems.at[at], semr.at[at], north)
        to_s = rcopy(src_s, dst_from_n, sems.at[at + 1], semr.at[at + 1], south)

        @pl.when(has_n)
        def _():
            to_n.start()

        @pl.when(has_s)
        def _():
            to_s.start()

        def finish():
            @pl.when(has_s)
            def _():
                to_n.wait_recv()
                to_s.wait_send()

            @pl.when(has_n)
            def _():
                to_s.wait_recv()
                to_n.wait_send()
        return finish

    lane8 = lanes((LV, NY))

    def pack_lat(slot, cells):
        to_n = jnp.zeros((LV, NY), F32)
        to_s = jnp.zeros((LV, NY), F32)
        for i, (m, e) in enumerate(cells):
            mine = (lane8 >= 5 * i) & (lane8 < 5 * i + 5)
            to_n = jnp.where(mine, roll(jnp.where(lane8 == 0, e, m), 5 * i + 4), to_n)
            to_s = jnp.where(mine, roll(jnp.where(lane8 == NY - 1, e, m), 5 * i + 1), to_s)
        pk[0, slot] = to_n
        pk[1, slot] = to_s

    def send_lat(lo_, hi_, at):
        return lat_exchange(pk.at[0, lo_:hi_], pk.at[1, lo_:hi_], pr.at[0, lo_:hi_], pr.at[1, lo_:hi_],
                            lat_s, lat_r, at)

    def from_lat(slot, i):
        a = roll(pr[0, slot], -(5 * i + 4))
        b = roll(pr[1, slot], -(5 * i + 1))
        fix = jnp.where(lane8 == 0, a, jnp.where(lane8 == NY - 1, b, 0.0))
        ext = jnp.where(lane8 >= NY - 4, a, jnp.where(lane8 < 4, b, 0.0))
        return fix, ext

    def pack_rows(exts, fixes):
        acc = jnp.zeros((LV, NY), F32)
        for r in range(len(exts)):
            acc = jnp.where((lane8 >= 8 * r) & (lane8 < 8 * r + 8), roll(exts[r], 8 * r + 4), acc)
        for r in range(len(fixes)):
            acc = jnp.where((lane8 >= 40 + 2 * r) & (lane8 < 42 + 2 * r), roll(fixes[r], 41 + 2 * r), acc)
        return acc

    x_lat = lat_exchange(xe.at[0], xe.at[1], xh.at[0], xh.at[1], x_s, x_r, 0)

    zero8 = jnp.zeros((LV, NY), F32)
    for v in range(NV):
        fm[NC + v, M:M + NX] = jnp.transpose(st_ref[v], (1, 0, 2))

    @pl.loop(0, NV)
    def _(v):
        pack_lat(2 * NC + v, [(fm[NC + v, M + x], zero8) for x in range(NX)])

    q_lat = send_lat(2 * NC, NP, 4)

    x_lat()
    c_left = rcopy(xh, xc.at[1], cor_s.at[0], cor_r.at[0], left)
    c_right = rcopy(xh, xc.at[0], cor_s.at[1], cor_r.at[1], right)
    c_left.start()
    c_right.start()

    def inject(corners):
        xpos = lanes((CH, NY)) % NX
        kinds = []
        for side in range(2):
            b = 2 * side
            own = xh[side].astype(F32)
            t0, t2 = roll(own, 1), roll(own, -1)
            if corners:
                t0 = jnp.where(xpos == 0, roll(xc[0, side].astype(F32), -(NX - 1)), t0)
                t2 = jnp.where(xpos == NX - 1, roll(xc[1, side].astype(F32), NX - 1), t2)
            taps = jnp.concatenate([t0.astype(BF16), xh[side], t2.astype(BF16)], axis=0)
            e = jnp.dot(lhs1[0, b * CH:(b + 1) * CH, 0:3 * CH], taps, preferred_element_type=F32)
            e_hi = e.astype(BF16).astype(F32)
            kinds += [e_hi, e - e_hi]
        group = lanes((CH, NY)) // 32
        for lp in range(LV // 2):
            inj = jnp.zeros((CH, NY), F32)
            for kind in range(4):
                inj = jnp.where(group == kind, roll(kinds[kind], 32 * kind - 32 * lp), inj)
            lhs1[lp, CH:2 * CH, 3 * CH:] = inj.astype(BF16)
            if not corners:
                lhs1[lp, 0:CH, 3 * CH:] = jnp.zeros((CH, NY), BF16)
                lhs1[lp, 2 * CH:, 3 * CH:] = jnp.zeros((CH, NY), BF16)

    inject(False)

    q_lat()

    @pl.loop(0, NV)
    def _(v):
        exts = []
        for x in range(NX):
            _, ext = from_lat(2 * NC + v, x)
            fe[NC + v, M + x] = ext
            exts.append(ext)
        epk[0, NC + v] = pack_rows(exts[:4], [])
        epk[1, NC + v] = pack_rows(exts[-4:], [])

    q_copies = [
        rcopy(fm.at[NC:NF, M:M + 4], fm.at[NC:NF, M + NX:M + NX + 4], q_s.at[0], q_r.at[0], left),
        rcopy(fm.at[NC:NF, M + NX - 4:M + NX], fm.at[NC:NF, 0:4], q_s.at[1], q_r.at[1], right),
        rcopy(epk.at[0, NC:NF], epr.at[1, NC:NF], q_s.at[2], q_r.at[2], left),
        rcopy(epk.at[1, NC:NF], epr.at[0, NC:NF], q_s.at[3], q_r.at[3], right)]
    for c in q_copies:
        c.start()

    lane1 = lanes((CH, NY))

    def conv1(lp, x):
        rhs = jnp.concatenate(
            [xt[2 * lp + h, pl.ds(x, 3)].reshape(3 * CH, NY) for h in range(2)], axis=1)
        rhs = jnp.concatenate([rhs, oh[x]], axis=0)
        s = jnp.dot(lhs1[lp], rhs, preferred_element_type=F32)
        for h in range(2):
            c = slice(h * NY, (h + 1) * NY)
            pre = s[CH:2 * CH, c] + bias[...]
            pre = pre + jnp.where(lane1 == 0, 0.0, roll(s[0:CH, c], 1))
            pre = pre + jnp.where(lane1 == NY - 1, 0.0, roll(s[2 * CH:, c], -1))
            half_pre = 0.5 * pre
            ht[2 * lp + h, x + 1] = (half_pre + half_pre * jnp.tanh(half_pre)).astype(BF16)

    lane64 = lanes((64, NY))

    def conv2(lp, j):
        rhs = jnp.concatenate(
            [ht[2 * lp + h, 2 * j:2 * j + 2].reshape(2 * CH, NY) for h in range(2)], axis=1)
        s = jnp.dot(lhs2[...], rhs, preferred_element_type=F32)
        out = []
        for h in range(2):
            c = slice(h * NY, (h + 1) * NY)
            up = roll(s[0:64, c], 1)
            dn = roll(s[128:192, c], -1)
            main = s[64:128, c] + jnp.where(lane64 == 0, 0.0, up) + jnp.where(lane64 == NY - 1, 0.0, dn)
            edge = jnp.where(lane64 == 0, up, 0.0) + jnp.where(lane64 == NY - 1, dn, 0.0)
            out.append((main, edge))
        return out

    def put(lp, row, parts, more=False):
        for h in range(2):
            at = pl.ds(row * (NC * LV) + 2 * lp + h, NC, stride=LV)
            for k, ref in enumerate((pm, pe)):
                t = None
                for pair, off in parts:
                    piece = pair[h][k][off * 16:off * 16 + NC]
                    t = piece if t is None else t + piece
                ref[at, :] = ref[at, :] + t if more else t

    def cell(row, f):
        at = pl.ds(pl.multiple_of((row * NC + f) * LV, LV), LV)
        return pm[at, :], pe[at, :]

    @pl.loop(0, LV)
    def _(i):
        lp, g = i // 2, i % 2
        for u in range(4):
            conv1(lp, 1 + 10 * g + u)

    for c in (c_left, c_right, *rows_left, *rows_right):
        c.wait()
    inject(True)

    @pl.loop(0, LV // 4)
    def _(i):
        for u in range(2):
            conv1(2 * i + u, 0)
            conv1(2 * i + u, NX - 1)

    @pl.loop(0, LV // 2)
    def _(lp):
        p = [conv2(lp, j) for j in range(3)]
        put(lp, 0, [(p[0], 1)])
        for i in range(2):
            put(lp, 1 + i, [(p[0], 2 + i), (p[1], i)])
            put(lp, 3 + i, [(p[1], 2 + i), (p[2], i)])
            put(lp, 5 + i, [(p[2], 2 + i)])
        p = [conv2(lp, j) for j in range(6, 9)]
        for i in range(2):
            put(lp, 11 + i, [(p[0], i)])
            put(lp, 13 + i, [(p[0], 2 + i), (p[1], i)])
            put(lp, 15 + i, [(p[1], 2 + i), (p[2], i)])
        put(lp, 17, [(p[2], 2)])

    span = 5 * NC * LV
    r_left = rcopy(pm.at[0:span], rowr.at[1], lon_s.at[0], lon_r.at[0], left)
    r_right = rcopy(pm.at[(NR - 5) * NC * LV:NR * NC * LV], rowr.at[0], lon_s.at[1], lon_r.at[1], right)
    r_left.start()
    r_right.start()

    outer = [0, 1, 2, 3, 4, NR - 5, NR - 4, NR - 3, NR - 2, NR - 1]
    inner = list(range(5, NR - 5))

    @pl.loop(0, NC)
    def _(f):
        pack_lat(f, [cell(r, f) for r in outer])

    outer_lat = send_lat(0, NC, 0)

    @pl.loop(0, LV // 2)
    def _(lp):
        for x in range(5, NX - 5):
            conv1(lp, x)

    outer_lat()

    def take(slot, i, row, f):
        m, e = cell(row, f)
        fix, ext = from_lat(slot, i)
        fm[f, M - 1 + row] = m + fix
        fe[f, M - 1 + row] = e + ext
        return fix, e + ext

    @pl.loop(0, NC)
    def _(f):
        got = [take(f, i, r, f) for i, r in enumerate(outer)]
        epk[0, f] = pack_rows([g[1] for g in got[:5]], [g[0] for g in got[:5]])
        epk[1, f] = pack_rows([g[1] for g in got[5:]], [g[0] for g in got[5:]])

    e_left = rcopy(epk.at[0, 0:NC], epr.at[1, 0:NC], lon_s.at[2], lon_r.at[2], left)
    e_right = rcopy(epk.at[1, 0:NC], epr.at[0, 0:NC], lon_s.at[3], lon_r.at[3], right)
    e_left.start()
    e_right.start()

    @pl.loop(0, LV // 2)
    def _(lp):
        p = [conv2(lp, j) for j in range(3, 6)]
        for i in range(2):
            put(lp, 5 + i, [(p[0], i)], True)
            put(lp, 7 + i, [(p[0], 2 + i), (p[1], i)])
            put(lp, 9 + i, [(p[1], 2 + i), (p[2], i)])
            put(lp, 11 + i, [(p[2], 2 + i)], True)

    @pl.loop(0, NC)
    def _(f):
        pack_lat(NC + f, [cell(r, f) for r in inner])

    inner_lat = send_lat(NC, 2 * NC, 2)

    for c in q_copies:
        c.wait()

    def ext_lanes(t):
        return jnp.where((lane8 < 4) | (lane8 >= NY - 4), t, 0.0)

    @pl.loop(NC, NF)
    def _(f):
        for side in range(2):
            t = epr[side, f]
            for r in range(4):
                fe[f, (0 if side == 0 else M + NX) + r] = ext_lanes(roll(t, -(8 * r + 4)))

    inner_lat()

    @pl.loop(0, NC)
    def _(f):
        for i, r in enumerate(inner):
            take(NC + f, i, r, f)

    for c in (r_left, r_right, e_left, e_right):
        c.wait()

    @pl.loop(0, NC)
    def _(f):
        for side in range(2):
            t = epr[side, f]
            for r in range(5):
                x = (r if side == 0 else M + NX - 1 + r)
                fix = jnp.where((lane8 == 0) | (lane8 == NY - 1), roll(t, -(41 + 2 * r)), 0.0)
                got = rowr[side, pl.ds(pl.multiple_of((r * NC + f) * LV, LV), LV), :] + fix
                ext = ext_lanes(roll(t, -(8 * r + 4)))
                if x < M - 1 or x > M + NX:
                    fm[f, x] = got
                    fe[f, x] = ext
                else:
                    fm[f, x] = fm[f, x] + got
                    fe[f, x] = fe[f, x] + ext

    cos_m = tab_ref[lat, 0, :, 0:NY]
    cos_e = tab_ref[lat, 0, :, NY:]
    cap_m = tab_ref[lat, 1, :, 0:NY]
    cap_e = tab_ref[lat, 1, :, NY:]
    met_m = 1.0 / cos_m
    met_e = 1.0 / cos_e

    def shift(m, e, step):
        sh = 1 if step < 0 else -1
        edge = 0 if step < 0 else NY - 1
        rm, re = roll(m, sh), roll(e, sh)
        at = lanes(m.shape) == edge
        return jnp.where(at, re, rm), jnp.where(at, rm, re)

    @pl.loop(0, NV)
    def _(v):
        bu = b2_ref[2 * v]
        bv = b2_ref[2 * v + 1]
        um = cap_m * jnp.tanh(fm[2 * v] + bu)
        ue = cap_e * jnp.tanh(fe[2 * v] + bu)
        vm = cap_m * jnp.tanh(fm[2 * v + 1] + bv)
        ve = cap_e * jnp.tanh(fe[2 * v + 1] + bv)
        vel_ref[2 * v] = um[M:M + NX]
        vel_ref[2 * v + 1] = vm[M:M + NX]
        i = slice(1, EX - 1)
        fn_m, fn_e = shift(vm[i] * cos_m, ve[i] * cos_e, 1)
        fs_m, fs_e = shift(vm[i] * cos_m, ve[i] * cos_e, -1)

        def coef(u, vv, met, fn, fs):
            div = met * ((u[2:] - u[:-2]) * 0.5 + (fn - fs) * 0.5)
            up, un = met * jnp.maximum(u[i], 0.0), met * jnp.minimum(u[i], 0.0)
            vp, vn = jnp.maximum(vv[i], 0.0), jnp.minimum(vv[i], 0.0)
            return (un - up) + (vn - vp) - div, up, un, vp, vn

        cm = coef(um, vm, met_m, fn_m, fs_m)
        ce = coef(ue, ve, met_e, fn_e, fs_e)

        def rate(qm, qe, k):
            n = EX - 2 * k
            nm, ne = shift(qm[1:-1], qe[1:-1], 1)
            sm, se = shift(qm[1:-1], qe[1:-1], -1)

            def one(q, c, qn, qs):
                c0, up, un, vp, vn = (t[k - 1:k - 1 + n] for t in c)
                return c0 * q[1:-1] + up * q[:-2] - un * q[2:] + vp * qs - vn * qn
            return one(qm, cm, nm, sm), one(qe, ce, ne, se)

        qm = fm[NC + v]
        qe = fe[NC + v]
        r1m, r1e = rate(qm, qe, 1)
        tot = r1m[3:3 + NX]
        r2m, r2e = rate(qm[1:-1] + 0.25 * r1m, qe[1:-1] + 0.25 * r1e, 2)
        tot = tot + 2.0 * r2m[2:2 + NX]
        r3m, r3e = rate(qm[2:-2] + 0.25 * r2m, qe[2:-2] + 0.25 * r2e, 3)
        tot = tot + 2.0 * r3m[1:1 + NX]
        r4m, _ = rate(qm[3:-3] + 0.5 * r3m, qe[3:-3] + 0.5 * r3e, 4)
        tend_ref[v] = (tot + r4m) * (1.0 / 6.0)


def solution(mesh):
    n_lon, n_lat = mesh.shape["lon"], mesh.shape["lat"]
    tables = lat_tables(n_lat)

    def body(hidden_in, w1, b1, w2, b2, state):
        vmem = pl.BlockSpec(memory_space=pltpu.VMEM)
        dma = pltpu.SemaphoreType.DMA
        vel, tend = pl.pallas_call(
            functools.partial(kernel, n_lon, n_lat),
            out_shape=(jax.ShapeDtypeStruct((NC, NX, LV, NY), F32),
                       jax.ShapeDtypeStruct((NV, NX, LV, NY), F32)),
            in_specs=[pl.BlockSpec(memory_space=pl.ANY), vmem, vmem, vmem,
                      pl.BlockSpec(memory_space=pltpu.SMEM), vmem, vmem],
            out_specs=(vmem, vmem),
            scratch_shapes=[
                pltpu.VMEM((LV, CH, NX, NY), BF16),
                pltpu.VMEM((LV, NX + 2, CH, NY), BF16),
                pltpu.VMEM((LV, NX + 2, CH, NY), BF16),
                pltpu.VMEM((LV // 2, 3 * CH, 4 * CH), BF16),
                pltpu.VMEM((192, 2 * CH), BF16),
                pltpu.VMEM((NX, CH, 2 * NY), BF16),
                pltpu.VMEM((NX, CH, 2 * NY), BF16),
                pltpu.VMEM((CH, NY), F32),
                pltpu.VMEM((2, CH, NY), BF16),
                pltpu.VMEM((2, CH, NY), BF16),
                pltpu.VMEM((2, 2, CH, NY), BF16),
                pltpu.VMEM((NR * NC * LV, NY), F32),
                pltpu.VMEM((NR * NC * LV, NY), F32),
                pltpu.VMEM((NF, EX, LV, NY), F32),
                pltpu.VMEM((NF, EX, LV, NY), F32),
                pltpu.VMEM((2, NP, LV, NY), F32),
                pltpu.VMEM((2, NP, LV, NY), F32),
                pltpu.VMEM((2, 5 * NC * LV, NY), F32),
                pltpu.VMEM((2, NF, LV, NY), F32),
                pltpu.VMEM((2, NF, LV, NY), F32),
                dma((LV,)), dma((2,)), dma((2,)), dma((4,)), dma((4,)), dma((2,)), dma((2,)),
                dma((6,)), dma((6,)), dma((4,)), dma((4,)), dma((4,)), dma((4,)),
            ],
            compiler_params=pltpu.CompilerParams(
                collective_id=0, has_side_effects=True, vmem_limit_bytes=55 * 1024 * 1024),
        )(hidden_in, w1, b1.reshape(1, CH), jnp.transpose(w2, (0, 1, 3, 2)), b2, state,
          jnp.asarray(tables))
        return jnp.transpose(vel, (0, 2, 1, 3)), jnp.transpose(tend, (0, 2, 1, 3))

    spread = P(None, None, "lon", "lat")
    return jax.shard_map(
        body, mesh=mesh, in_specs=(spread, P(), P(), P(), P(), spread),
        out_specs=(spread, spread), check_vma=False)
```

```python
import functools
import math

import jax
import jax.numpy as jnp
import numpy as np
from jax import lax
from jax.experimental import pallas as pl
from jax.experimental.pallas import tpu as pltpu
from jax.sharding import PartitionSpec as P

MESH = pl.DeviceIdType.MESH
F32 = jnp.float32
BF16 = jnp.bfloat16
TIME_STEP = 0.5
SPEED_CAP = 0.6
COS_FLOOR = 0.5
NV = 6
NC = 12
NF = 18
LV = 8
NX = 16
NY = 128
CH = 128
M = 4
EX = NX + 2 * M
NR = NX + 2
NP = 2 * NC + NV
HALF = LV // 2


def lat_tables(n_lat_dev):
    n_lat = n_lat_dev * NY
    out = np.zeros((n_lat_dev, 2, LV, 2 * NY), np.float32)
    for d in range(n_lat_dev):
        lane = np.arange(2 * NY)
        y = np.where(lane < NY + NY // 2, lane, lane - 2 * NY) + d * NY
        phi = (y + 0.5) * (math.pi / n_lat) - 0.5 * math.pi
        inside = ((y >= 0) & (y < n_lat)).astype(np.float32)
        out[d, 0] = np.maximum(np.cos(phi), COS_FLOOR)[None]
        out[d, 1] = (SPEED_CAP * inside)[None]
    return out


def lanes(shape):
    return lax.broadcasted_iota(jnp.int32, shape, len(shape) - 1)


def roll(v, s):
    s = s % NY
    return v if s == 0 else pltpu.roll(v, s, v.ndim - 1)


def kernel(n_lon, n_lat, x_hbm, w1_ref, b1_ref, w2_ref, b2_ref, st_ref, tab_ref,
           vel_ref, tend_ref,
           xin, xt, ht, lhs1, lhs2, oh, ohe, bias, xe, xh, xc, pm, pe, fm, fe, pk, pr, rowr, epk, epr,
           in_sem, x_s, x_r, row_s, row_r, cor_s, cor_r, lat_s, lat_r, lon_s, lon_r, q_s, q_r):
    lon = lax.axis_index("lon")
    lat = lax.axis_index("lat")
    left = (lax.rem(lon + n_lon - 1, n_lon), lat)
    right = (lax.rem(lon + 1, n_lon), lat)
    south = (lon, lat - 1)
    north = (lon, lat + 1)
    has_s = lat > 0
    has_n = lat < n_lat - 1

    for side, has in ((0, has_s), (1, has_n)):
        @pl.when(jnp.logical_not(has))
        def _():
            xh[side] = jnp.zeros((CH, NY), BF16)
            pr[side] = jnp.zeros((NP, LV, NY), F32)

    barrier = pltpu.get_barrier_semaphore()
    for dev in (left, right):
        pl.semaphore_signal(barrier, inc=1, device_id=dev, device_id_type=MESH)

    @pl.when(has_s)
    def _():
        pl.semaphore_signal(barrier, inc=1, device_id=south, device_id_type=MESH)

    @pl.when(has_n)
    def _():
        pl.semaphore_signal(barrier, inc=1, device_id=north, device_id_type=MESH)

    loads = [pltpu.make_async_copy(x_hbm.at[l], xin.at[l], in_sem.at[l]) for l in range(LV)]
    for c in loads:
        c.start()

    for b in range(3):
        for a in range(3):
            lhs1[0, b * CH:(b + 1) * CH, a * CH:(a + 1) * CH] = jnp.transpose(w1_ref[a, b], (1, 0))
    for lp in range(1, LV // 2):
        lhs1[lp, :, 0:3 * CH] = lhs1[0, :, 0:3 * CH]
    lhs2[...] = jnp.zeros_like(lhs2)
    for b in range(3):
        for off in range(4):
            for r in range(2):
                a = r - off + 2
                if 0 <= a <= 2:
                    base = b * 64 + off * 16
                    lhs2[base:base + NC, r * CH:(r + 1) * CH] = w2_ref[a, b]
    bias[...] = jnp.transpose(jnp.broadcast_to(b1_ref[...], (CH, CH)), (1, 0))
    k_id = lax.broadcasted_iota(jnp.int32, (CH, 2 * NY), 0)
    lane2 = lanes((CH, 2 * NY))
    half = (k_id // 16) % 2
    target = half * NY + jnp.where(k_id < 64, 0, NY - 1)
    hit = lane2 == target

    @pl.loop(0, NX)
    def _(x):
        oh[x] = jnp.where(hit & (k_id % 16 == x), 1.0, 0.0).astype(BF16)
        want_hi = (k_id == NY - 1) & (lane2 == x)
        want_lo = (k_id == 0) & (lane2 == NY + x)
        ohe[x] = jnp.where(want_hi | want_lo, 1.0, 0.0).astype(BF16)

    ht[:, 0] = jnp.zeros((LV, CH, NY), BF16)
    ht[:, NX + 1] = jnp.zeros((LV, CH, NY), BF16)

    def rcopy(src, dst, ss, rs_, dev):
        return pltpu.make_async_remote_copy(src_ref=src, dst_ref=dst, send_sem=ss, recv_sem=rs_,
                                            device_id=dev, device_id_type=MESH)

    hi = jnp.zeros((CH, NY), F32)
    lo = jnp.zeros((CH, NY), F32)
    rows_left, rows_right = [], []
    for l in range(LV):
        loads[l].wait()
        xt[l, 1:NX + 1] = jnp.transpose(xin[l], (1, 0, 2))
        if l % 2 == 1:
            row = jnp.concatenate(
                [jnp.concatenate([xt[l - 1 + h, 1 + x] for x in range(NX)], axis=1) for h in range(2)], axis=0)
            res = jnp.dot(row, ohe[...].reshape(NX * NY, 2 * NY), preferred_element_type=F32)
            for h in range(2):
                hi = hi + roll(res[h * CH:(h + 1) * CH, :NY], 16 * (l - 1 + h))
                lo = lo + roll(res[h * CH:(h + 1) * CH, NY:], 16 * (l - 1 + h))
        if l == HALF - 1:
            pl.semaphore_wait(barrier, 2 + has_s.astype(jnp.int32) + has_n.astype(jnp.int32))
        if (l + 1) % HALF == 0:
            g = l // HALF
            part = slice(g * HALF, (g + 1) * HALF)
            rows_left.append(rcopy(xt.at[part, 1], xt.at[part, NX + 1], row_s.at[g], row_r.at[g], left))
            rows_right.append(rcopy(xt.at[part, NX], xt.at[part, 0], row_s.at[2 + g], row_r.at[2 + g], right))
            if g == 0:
                rows_left[0].start()
                rows_right[0].start()
    xe[0] = hi.astype(BF16)
    xe[1] = lo.astype(BF16)

    def lat_exchange(src_n, src_s, dst_from_s, dst_from_n, sems, semr, at):
        to_n = rcopy(src_n, dst_from_s, sems.at[at], semr.at[at], north)
        to_s = rcopy(src_s, dst_from_n, sems.at[at + 1], semr.at[at + 1], south)

        @pl.when(has_n)
        def _():
            to_n.start()

        @pl.when(has_s)
        def _():
            to_s.start()

        def finish():
            @pl.when(has_s)
            def _():
                to_n.wait_recv()
                to_s.wait_send()

            @pl.when(has_n)
            def _():
                to_s.wait_recv()
                to_n.wait_send()
        return finish

    lane8 = lanes((LV, NY))

    def pack_lat(slot, cells):
        to_n = jnp.zeros((LV, NY), F32)
        to_s = jnp.zeros((LV, NY), F32)
        for i, (m, e) in enumerate(cells):
            mine = (lane8 >= 5 * i) & (lane8 < 5 * i + 5)
            to_n = jnp.where(mine, roll(jnp.where(lane8 == 0, e, m), 5 * i + 4), to_n)
            to_s = jnp.where(mine, roll(jnp.where(lane8 == NY - 1, e, m), 5 * i + 1), to_s)
        pk[0, slot] = to_n
        pk[1, slot] = to_s

    def send_lat(lo_, hi_, at):
        return lat_exchange(pk.at[0, lo_:hi_], pk.at[1, lo_:hi_], pr.at[0, lo_:hi_], pr.at[1, lo_:hi_],
                            lat_s, lat_r, at)

    def from_lat(slot, i):
        a = roll(pr[0, slot], -(5 * i + 4))
        b = roll(pr[1, slot], -(5 * i + 1))
        fix = jnp.where(lane8 == 0, a, jnp.where(lane8 == NY - 1, b, 0.0))
        ext = jnp.where(lane8 >= NY - 4, a, jnp.where(lane8 < 4, b, 0.0))
        return fix, ext

    def pack_rows(exts, fixes):
        acc = jnp.zeros((LV, NY), F32)
        for r in range(len(exts)):
            acc = jnp.where((lane8 >= 8 * r) & (lane8 < 8 * r + 8), roll(exts[r], 8 * r + 4), acc)
        for r in range(len(fixes)):
            acc = jnp.where((lane8 >= 40 + 2 * r) & (lane8 < 42 + 2 * r), roll(fixes[r], 41 + 2 * r), acc)
        return acc

    x_lat = lat_exchange(xe.at[0], xe.at[1], xh.at[0], xh.at[1], x_s, x_r, 0)

    zero8 = jnp.zeros((LV, NY), F32)
    for v in range(NV):
        fm[NC + v, M:M + NX] = jnp.transpose(st_ref[v], (1, 0, 2))

    @pl.loop(0, NV, unroll=2)
    def _(v):
        pack_lat(2 * NC + v, [(fm[NC + v, M + x], zero8) for x in range(NX)])

    x_lat()
    c_left = rcopy(xh, xc.at[1], cor_s.at[0], cor_r.at[0], left)
    c_right = rcopy(xh, xc.at[0], cor_s.at[1], cor_r.at[1], right)
    c_left.start()
    c_right.start()
    rows_left[1].start()
    rows_right[1].start()
    q_copies = [
        rcopy(fm.at[NC:NF, M:M + 4], fm.at[NC:NF, M + NX:M + NX + 4], q_s.at[0], q_r.at[0], left),
        rcopy(fm.at[NC:NF, M + NX - 4:M + NX], fm.at[NC:NF, 0:4], q_s.at[1], q_r.at[1], right)]
    for c in q_copies:
        c.start()

    def inject(corners):
        xpos = lanes((CH, NY)) % NX
        kinds = []
        for side in range(2):
            b = 2 * side
            own = xh[side].astype(F32)
            t0, t2 = roll(own, 1), roll(own, -1)
            if corners:
                t0 = jnp.where(xpos == 0, roll(xc[0, side].astype(F32), -(NX - 1)), t0)
                t2 = jnp.where(xpos == NX - 1, roll(xc[1, side].astype(F32), NX - 1), t2)
            taps = jnp.concatenate([t0.astype(BF16), xh[side], t2.astype(BF16)], axis=0)
            e = jnp.dot(lhs1[0, b * CH:(b + 1) * CH, 0:3 * CH], taps, preferred_element_type=F32)
            e_hi = e.astype(BF16).astype(F32)
            kinds += [e_hi, e - e_hi]
        group = lanes((CH, NY)) // 32
        for lp in range(LV // 2):
            inj = jnp.zeros((CH, NY), F32)
            for kind in range(4):
                inj = jnp.where(group == kind, roll(kinds[kind], 32 * kind - 32 * lp), inj)
            lhs1[lp, CH:2 * CH, 3 * CH:] = inj.astype(BF16)
            if not corners:
                lhs1[lp, 0:CH, 3 * CH:] = jnp.zeros((CH, NY), BF16)
                lhs1[lp, 2 * CH:, 3 * CH:] = jnp.zeros((CH, NY), BF16)

    inject(False)

    q_lat = send_lat(2 * NC, NP, 4)

    lane1 = lanes((CH, NY))

    def conv1(lp, x):
        rhs = jnp.concatenate(
            [xt[2 * lp + h, pl.ds(x, 3)].reshape(3 * CH, NY) for h in range(2)], axis=1)
        rhs = jnp.concatenate([rhs, oh[x]], axis=0)
        s = jnp.dot(lhs1[lp], rhs, preferred_element_type=F32)
        for h in range(2):
            c = slice(h * NY, (h + 1) * NY)
            pre = s[CH:2 * CH, c] + bias[...]
            pre = pre + jnp.where(lane1 == 0, 0.0, roll(s[0:CH, c], 1))
            pre = pre + jnp.where(lane1 == NY - 1, 0.0, roll(s[2 * CH:, c], -1))
            half_pre = 0.5 * pre
            ht[2 * lp + h, x + 1] = (half_pre + half_pre * jnp.tanh(half_pre)).astype(BF16)

    lane64 = lanes((64, NY))

    def conv2(lp, j):
        rhs = jnp.concatenate(
            [ht[2 * lp + h, 2 * j:2 * j + 2].reshape(2 * CH, NY) for h in range(2)], axis=1)
        s = jnp.dot(lhs2[...], rhs, preferred_element_type=F32)
        out = []
        for h in range(2):
            c = slice(h * NY, (h + 1) * NY)
            up = roll(s[0:64, c], 1)
            dn = roll(s[128:192, c], -1)
            main = s[64:128, c] + jnp.where(lane64 == 0, 0.0, up) + jnp.where(lane64 == NY - 1, 0.0, dn)
            edge = jnp.where(lane64 == 0, up, 0.0) + jnp.where(lane64 == NY - 1, dn, 0.0)
            out.append((main, edge))
        return out

    def put(lp, row, parts, more=False):
        for h in range(2):
            at = pl.ds(row * (NC * LV) + 2 * lp + h, NC, stride=LV)
            for k, ref in enumerate((pm, pe)):
                t = None
                for pair, off in parts:
                    piece = pair[h][k][off * 16:off * 16 + NC]
                    t = piece if t is None else t + piece
                ref[at, :] = ref[at, :] + t if more else t

    def cell(row, f):
        at = pl.ds(pl.multiple_of((row * NC + f) * LV, LV), LV)
        return pm[at, :], pe[at, :]

    @pl.loop(0, LV)
    def _(i):
        lp, g = i // 2, i % 2
        for u in range(4):
            conv1(lp, 1 + 10 * g + u)

    for c in (c_left, c_right, *rows_left, *rows_right):
        c.wait()
    inject(True)

    @pl.loop(0, LV // 4)
    def _(i):
        for u in range(2):
            conv1(2 * i + u, 0)
            conv1(2 * i + u, NX - 1)

    q_lat()

    @pl.loop(0, NV, unroll=2)
    def _(v):
        exts = []
        for x in range(NX):
            _, ext = from_lat(2 * NC + v, x)
            fe[NC + v, M + x] = ext
            exts.append(ext)
        epk[0, NC + v] = pack_rows(exts[:4], [])
        epk[1, NC + v] = pack_rows(exts[-4:], [])

    q_edges = [
        rcopy(epk.at[0, NC:NF], epr.at[1, NC:NF], q_s.at[2], q_r.at[2], left),
        rcopy(epk.at[1, NC:NF], epr.at[0, NC:NF], q_s.at[3], q_r.at[3], right)]
    for c in q_edges:
        c.start()

    @pl.loop(0, LV // 2)
    def _(lp):
        p = [conv2(lp, j) for j in range(3)]
        put(lp, 0, [(p[0], 1)])
        for i in range(2):
            put(lp, 1 + i, [(p[0], 2 + i), (p[1], i)])
            put(lp, 3 + i, [(p[1], 2 + i), (p[2], i)])
            put(lp, 5 + i, [(p[2], 2 + i)])
        p = [conv2(lp, j) for j in range(6, 9)]
        for i in range(2):
            put(lp, 11 + i, [(p[0], i)])
            put(lp, 13 + i, [(p[0], 2 + i), (p[1], i)])
            put(lp, 15 + i, [(p[1], 2 + i), (p[2], i)])
        put(lp, 17, [(p[2], 2)])

    def rows_part(k, lo_, hi_):
        at, to = pl.ds(lo_ * NC * LV, (hi_ - lo_) * NC * LV), NR - 5
        far = pl.ds((to + lo_) * NC * LV, (hi_ - lo_) * NC * LV)
        return [rcopy(pm.at[at], rowr.at[1, at], lon_s.at[k], lon_r.at[k], left),
                rcopy(pm.at[far], rowr.at[0, at], lon_s.at[k + 1], lon_r.at[k + 1], right)]

    first_rows = rows_part(0, 0, 2)
    last_rows = rows_part(4, 2, 5)
    for c in first_rows:
        c.start()

    outer = [0, 1, 2, 3, 4, NR - 5, NR - 4, NR - 3, NR - 2, NR - 1]
    inner = list(range(5, NR - 5))

    @pl.loop(0, NC, unroll=2)
    def _(f):
        pack_lat(f, [cell(r, f) for r in outer])

    outer_lat = send_lat(0, NC, 0)

    @pl.loop(0, LV // 2)
    def _(lp):
        for x in range(5, NX - 7):
            conv1(lp, x)

    outer_lat()
    for c in last_rows:
        c.start()

    @pl.loop(0, LV // 4)
    def _(i):
        for u in range(2):
            for x in range(NX - 7, NX - 5):
                conv1(2 * i + u, x)

    def take(slot, i, row, f):
        m, e = cell(row, f)
        fix, ext = from_lat(slot, i)
        fm[f, M - 1 + row] = m + fix
        fe[f, M - 1 + row] = e + ext
        return fix, e + ext

    @pl.loop(0, NC, unroll=2)
    def _(f):
        got = [take(f, i, r, f) for i, r in enumerate(outer)]
        epk[0, f] = pack_rows([g[1] for g in got[:5]], [g[0] for g in got[:5]])
        epk[1, f] = pack_rows([g[1] for g in got[5:]], [g[0] for g in got[5:]])

    e_left = rcopy(epk.at[0, 0:NC], epr.at[1, 0:NC], lon_s.at[2], lon_r.at[2], left)
    e_right = rcopy(epk.at[1, 0:NC], epr.at[0, 0:NC], lon_s.at[3], lon_r.at[3], right)
    e_left.start()
    e_right.start()

    @pl.loop(0, LV // 2)
    def _(lp):
        p = [conv2(lp, j) for j in range(3, 6)]
        for i in range(2):
            put(lp, 5 + i, [(p[0], i)], True)
            put(lp, 7 + i, [(p[0], 2 + i), (p[1], i)])
            put(lp, 9 + i, [(p[1], 2 + i), (p[2], i)])
            put(lp, 11 + i, [(p[2], 2 + i)], True)

    @pl.loop(0, NC, unroll=2)
    def _(f):
        pack_lat(NC + f, [cell(r, f) for r in inner])

    inner_lat = send_lat(NC, 2 * NC, 2)

    for c in (*q_copies, *q_edges):
        c.wait()

    def ext_lanes(t):
        return jnp.where((lane8 < 4) | (lane8 >= NY - 4), t, 0.0)

    @pl.loop(NC, NF)
    def _(f):
        for side in range(2):
            t = epr[side, f]
            for r in range(4):
                fe[f, (0 if side == 0 else M + NX) + r] = ext_lanes(roll(t, -(8 * r + 4)))

    inner_lat()

    @pl.loop(0, NC, unroll=2)
    def _(f):
        for i, r in enumerate(inner):
            take(NC + f, i, r, f)

    for c in (*first_rows, *last_rows, e_left, e_right):
        c.wait()

    @pl.loop(0, NC, unroll=2)
    def _(f):
        for side in range(2):
            t = epr[side, f]
            for r in range(5):
                x = (r if side == 0 else M + NX - 1 + r)
                fix = jnp.where((lane8 == 0) | (lane8 == NY - 1), roll(t, -(41 + 2 * r)), 0.0)
                got = rowr[side, pl.ds(pl.multiple_of((r * NC + f) * LV, LV), LV), :] + fix
                ext = ext_lanes(roll(t, -(8 * r + 4)))
                if x < M - 1 or x > M + NX:
                    fm[f, x] = got
                    fe[f, x] = ext
                else:
                    fm[f, x] = fm[f, x] + got
                    fe[f, x] = fe[f, x] + ext

    cos_m = tab_ref[lat, 0, :, 0:NY]
    cos_e = tab_ref[lat, 0, :, NY:]
    cap_m = tab_ref[lat, 1, :, 0:NY]
    cap_e = tab_ref[lat, 1, :, NY:]
    met_m = 1.0 / cos_m
    met_e = 1.0 / cos_e

    def shift(m, e, step):
        sh = 1 if step < 0 else -1
        edge = 0 if step < 0 else NY - 1
        rm, re = roll(m, sh), roll(e, sh)
        at = lanes(m.shape) == edge
        return jnp.where(at, re, rm), jnp.where(at, rm, re)

    @pl.loop(0, NV)
    def _(v):
        bu = b2_ref[2 * v]
        bv = b2_ref[2 * v + 1]
        um = cap_m * jnp.tanh(fm[2 * v] + bu)
        ue = cap_e * jnp.tanh(fe[2 * v] + bu)
        vm = cap_m * jnp.tanh(fm[2 * v + 1] + bv)
        ve = cap_e * jnp.tanh(fe[2 * v + 1] + bv)
        vel_ref[2 * v] = um[M:M + NX]
        vel_ref[2 * v + 1] = vm[M:M + NX]
        i = slice(1, EX - 1)
        fn_m, fn_e = shift(vm[i] * cos_m, ve[i] * cos_e, 1)
        fs_m, fs_e = shift(vm[i] * cos_m, ve[i] * cos_e, -1)

        def coef(u, vv, met, fn, fs):
            div = met * ((u[2:] - u[:-2]) * 0.5 + (fn - fs) * 0.5)
            up, un = met * jnp.maximum(u[i], 0.0), met * jnp.minimum(u[i], 0.0)
            vp, vn = jnp.maximum(vv[i], 0.0), jnp.minimum(vv[i], 0.0)
            return (un - up) + (vn - vp) - div, up, un, vp, vn

        cm = coef(um, vm, met_m, fn_m, fs_m)
        ce = coef(ue, ve, met_e, fn_e, fs_e)

        def rate(qm, qe, k):
            n = EX - 2 * k
            nm, ne = shift(qm[1:-1], qe[1:-1], 1)
            sm, se = shift(qm[1:-1], qe[1:-1], -1)

            def one(q, c, qn, qs):
                c0, up, un, vp, vn = (t[k - 1:k - 1 + n] for t in c)
                return c0 * q[1:-1] + up * q[:-2] - un * q[2:] + vp * qs - vn * qn
            return one(qm, cm, nm, sm), one(qe, ce, ne, se)

        qm = fm[NC + v]
        qe = fe[NC + v]
        r1m, r1e = rate(qm, qe, 1)
        tot = r1m[3:3 + NX]
        r2m, r2e = rate(qm[1:-1] + 0.25 * r1m, qe[1:-1] + 0.25 * r1e, 2)
        tot = tot + 2.0 * r2m[2:2 + NX]
        r3m, r3e = rate(qm[2:-2] + 0.25 * r2m, qe[2:-2] + 0.25 * r2e, 3)
        tot = tot + 2.0 * r3m[1:1 + NX]
        r4m, _ = rate(qm[3:-3] + 0.5 * r3m, qe[3:-3] + 0.5 * r3e, 4)
        tend_ref[v] = (tot + r4m) * (1.0 / 6.0)


def solution(mesh):
    n_lon, n_lat = mesh.shape["lon"], mesh.shape["lat"]
    tables = lat_tables(n_lat)

    def body(hidden_in, w1, b1, w2, b2, state):
        vmem = pl.BlockSpec(memory_space=pltpu.VMEM)
        dma = pltpu.SemaphoreType.DMA
        vel, tend = pl.pallas_call(
            functools.partial(kernel, n_lon, n_lat),
            out_shape=(jax.ShapeDtypeStruct((NC, NX, LV, NY), F32),
                       jax.ShapeDtypeStruct((NV, NX, LV, NY), F32)),
            in_specs=[pl.BlockSpec(memory_space=pl.ANY), vmem, vmem, vmem,
                      pl.BlockSpec(memory_space=pltpu.SMEM), vmem, vmem],
            out_specs=(vmem, vmem),
            scratch_shapes=[
                pltpu.VMEM((LV, CH, NX, NY), BF16),
                pltpu.VMEM((LV, NX + 2, CH, NY), BF16),
                pltpu.VMEM((LV, NX + 2, CH, NY), BF16),
                pltpu.VMEM((LV // 2, 3 * CH, 4 * CH), BF16),
                pltpu.VMEM((192, 2 * CH), BF16),
                pltpu.VMEM((NX, CH, 2 * NY), BF16),
                pltpu.VMEM((NX, CH, 2 * NY), BF16),
                pltpu.VMEM((CH, NY), F32),
                pltpu.VMEM((2, CH, NY), BF16),
                pltpu.VMEM((2, CH, NY), BF16),
                pltpu.VMEM((2, 2, CH, NY), BF16),
                pltpu.VMEM((NR * NC * LV, NY), F32),
                pltpu.VMEM((NR * NC * LV, NY), F32),
                pltpu.VMEM((NF, EX, LV, NY), F32),
                pltpu.VMEM((NF, EX, LV, NY), F32),
                pltpu.VMEM((2, NP, LV, NY), F32),
                pltpu.VMEM((2, NP, LV, NY), F32),
                pltpu.VMEM((2, 5 * NC * LV, NY), F32),
                pltpu.VMEM((2, NF, LV, NY), F32),
                pltpu.VMEM((2, NF, LV, NY), F32),
                dma((LV,)), dma((2,)), dma((2,)), dma((4,)), dma((4,)), dma((2,)), dma((2,)),
                dma((6,)), dma((6,)), dma((6,)), dma((6,)), dma((4,)), dma((4,)),
            ],
            compiler_params=pltpu.CompilerParams(
                collective_id=0, has_side_effects=True, vmem_limit_bytes=55 * 1024 * 1024),
        )(hidden_in, w1, b1.reshape(1, CH), jnp.transpose(w2, (0, 1, 3, 2)), b2, state,
          jnp.asarray(tables))
        return jnp.transpose(vel, (0, 2, 1, 3)), jnp.transpose(tend, (0, 2, 1, 3))

    spread = P(None, None, "lon", "lat")
    return jax.shard_map(
        body, mesh=mesh, in_specs=(spread, P(), P(), P(), P(), spread),
        out_specs=(spread, spread), check_vma=False)
```

```python
import functools
import math

import jax
import jax.numpy as jnp
import numpy as np
from jax import lax
from jax.experimental import pallas as pl
from jax.experimental.pallas import tpu as pltpu
from jax.sharding import PartitionSpec as P

MESH = pl.DeviceIdType.MESH
F32 = jnp.float32
BF16 = jnp.bfloat16
TIME_STEP = 0.5
SPEED_CAP = 0.6
COS_FLOOR = 0.5
NV = 6
NC = 12
NF = 18
LV = 8
NX = 16
NY = 128
CH = 128
M = 4
EX = NX + 2 * M
NR = NX + 2
NP = 2 * NC + NV
HALF = LV // 2


def lat_tables(n_lat_dev):
    n_lat = n_lat_dev * NY
    out = np.zeros((n_lat_dev, 2, LV, 2 * NY), np.float32)
    for d in range(n_lat_dev):
        lane = np.arange(2 * NY)
        y = np.where(lane < NY + NY // 2, lane, lane - 2 * NY) + d * NY
        phi = (y + 0.5) * (math.pi / n_lat) - 0.5 * math.pi
        inside = ((y >= 0) & (y < n_lat)).astype(np.float32)
        out[d, 0] = np.maximum(np.cos(phi), COS_FLOOR)[None]
        out[d, 1] = (SPEED_CAP * inside)[None]
    return out


def lanes(shape):
    return lax.broadcasted_iota(jnp.int32, shape, len(shape) - 1)


def roll(v, s):
    s = s % NY
    return v if s == 0 else pltpu.roll(v, s, v.ndim - 1)


def kernel(n_lon, n_lat, x_hbm, w1_hbm, b1_hbm, w2_hbm, b2_ref, st_hbm, tab_hbm,
           vel_ref, tend_ref,
           w1_ref, b1_ref, w2_ref, st_ref, tab_ref, arg_sem, xin, xt, ht, lhs1, lhs2, oh, ohe, bias, xe, xh, xc, pm, pe, fm, fe, pk, pr, rowr, epk, epr,
           in_sem, x_s, x_r, row_s, row_r, cor_s, cor_r, lat_s, lat_r, lon_s, lon_r, q_s, q_r):
    lon = lax.axis_index("lon")
    lat = lax.axis_index("lat")
    left = (lax.rem(lon + n_lon - 1, n_lon), lat)
    right = (lax.rem(lon + 1, n_lon), lat)
    south = (lon, lat - 1)
    north = (lon, lat + 1)
    has_s = lat > 0
    has_n = lat < n_lat - 1

    for side, has in ((0, has_s), (1, has_n)):
        @pl.when(jnp.logical_not(has))
        def _():
            xh[side] = jnp.zeros((CH, NY), BF16)
            pr[side] = jnp.zeros((NP, LV, NY), F32)

    barrier = pltpu.get_barrier_semaphore()
    for dev in (left, right):
        pl.semaphore_signal(barrier, inc=1, device_id=dev, device_id_type=MESH)

    @pl.when(has_s)
    def _():
        pl.semaphore_signal(barrier, inc=1, device_id=south, device_id_type=MESH)

    @pl.when(has_n)
    def _():
        pl.semaphore_signal(barrier, inc=1, device_id=north, device_id_type=MESH)

    loads = [pltpu.make_async_copy(x_hbm.at[l], xin.at[l], in_sem.at[l]) for l in range(LV)]
    args = [pltpu.make_async_copy(src, dst, arg_sem.at[i]) for i, (src, dst) in enumerate(
        ((w1_hbm, w1_ref), (w2_hbm, w2_ref), (b1_hbm, b1_ref), (st_hbm, st_ref), (tab_hbm, tab_ref)))]
    for c in (*args[:3], *loads, *args[3:]):
        c.start()

    k_id = lax.broadcasted_iota(jnp.int32, (CH, 2 * NY), 0)
    lane2 = lanes((CH, 2 * NY))
    half = (k_id // 16) % 2
    target = half * NY + jnp.where(k_id < 64, 0, NY - 1)
    hit = lane2 == target

    @pl.loop(0, NX)
    def _(x):
        oh[x] = jnp.where(hit & (k_id % 16 == x), 1.0, 0.0).astype(BF16)
        want_hi = (k_id == NY - 1) & (lane2 == x)
        want_lo = (k_id == 0) & (lane2 == NY + x)
        ohe[x] = jnp.where(want_hi | want_lo, 1.0, 0.0).astype(BF16)

    for c in args[:3]:
        c.wait()
    for b in range(3):
        for a in range(3):
            lhs1[0, b * CH:(b + 1) * CH, a * CH:(a + 1) * CH] = jnp.transpose(w1_ref[a, b], (1, 0))
    for lp in range(1, LV // 2):
        lhs1[lp, :, 0:3 * CH] = lhs1[0, :, 0:3 * CH]
    lhs2[...] = jnp.zeros_like(lhs2)
    for b in range(3):
        for off in range(4):
            for r in range(2):
                a = r - off + 2
                if 0 <= a <= 2:
                    base = b * 64 + off * 16
                    lhs2[base:base + NC, r * CH:(r + 1) * CH] = w2_ref[a, b]
    bias[...] = jnp.transpose(jnp.broadcast_to(b1_ref[...], (CH, CH)), (1, 0))
    ht[:, 0] = jnp.zeros((LV, CH, NY), BF16)
    ht[:, NX + 1] = jnp.zeros((LV, CH, NY), BF16)

    def rcopy(src, dst, ss, rs_, dev):
        return pltpu.make_async_remote_copy(src_ref=src, dst_ref=dst, send_sem=ss, recv_sem=rs_,
                                            device_id=dev, device_id_type=MESH)

    hi = jnp.zeros((CH, NY), F32)
    lo = jnp.zeros((CH, NY), F32)
    rows_left, rows_right = [], []
    for l in range(LV):
        loads[l].wait()
        xt[l, 1:NX + 1] = jnp.transpose(xin[l], (1, 0, 2))
        if l % 2 == 1:
            row = jnp.concatenate(
                [jnp.concatenate([xt[l - 1 + h, 1 + x] for x in range(NX)], axis=1) for h in range(2)], axis=0)
            res = jnp.dot(row, ohe[...].reshape(NX * NY, 2 * NY), preferred_element_type=F32)
            for h in range(2):
                hi = hi + roll(res[h * CH:(h + 1) * CH, :NY], 16 * (l - 1 + h))
                lo = lo + roll(res[h * CH:(h + 1) * CH, NY:], 16 * (l - 1 + h))
        if l == HALF - 1:
            pl.semaphore_wait(barrier, 2 + has_s.astype(jnp.int32) + has_n.astype(jnp.int32))
        if (l + 1) % HALF == 0:
            g = l // HALF
            part = slice(g * HALF, (g + 1) * HALF)
            rows_left.append(rcopy(xt.at[part, 1], xt.at[part, NX + 1], row_s.at[g], row_r.at[g], left))
            rows_right.append(rcopy(xt.at[part, NX], xt.at[part, 0], row_s.at[2 + g], row_r.at[2 + g], right))
            if g == 0:
                rows_left[0].start()
                rows_right[0].start()
    xe[0] = hi.astype(BF16)
    xe[1] = lo.astype(BF16)

    def lat_exchange(src_n, src_s, dst_from_s, dst_from_n, sems, semr, at):
        to_n = rcopy(src_n, dst_from_s, sems.at[at], semr.at[at], north)
        to_s = rcopy(src_s, dst_from_n, sems.at[at + 1], semr.at[at + 1], south)

        @pl.when(has_n)
        def _():
            to_n.start()

        @pl.when(has_s)
        def _():
            to_s.start()

        def finish():
            @pl.when(has_s)
            def _():
                to_n.wait_recv()
                to_s.wait_send()

            @pl.when(has_n)
            def _():
                to_s.wait_recv()
                to_n.wait_send()
        return finish

    lane8 = lanes((LV, NY))

    def pack_lat(slot, cells):
        to_n = jnp.zeros((LV, NY), F32)
        to_s = jnp.zeros((LV, NY), F32)
        for i, (m, e) in enumerate(cells):
            mine = (lane8 >= 5 * i) & (lane8 < 5 * i + 5)
            to_n = jnp.where(mine, roll(jnp.where(lane8 == 0, e, m), 5 * i + 4), to_n)
            to_s = jnp.where(mine, roll(jnp.where(lane8 == NY - 1, e, m), 5 * i + 1), to_s)
        pk[0, slot] = to_n
        pk[1, slot] = to_s

    def send_lat(lo_, hi_, at):
        return lat_exchange(pk.at[0, lo_:hi_], pk.at[1, lo_:hi_], pr.at[0, lo_:hi_], pr.at[1, lo_:hi_],
                            lat_s, lat_r, at)

    def from_lat(slot, i):
        a = roll(pr[0, slot], -(5 * i + 4))
        b = roll(pr[1, slot], -(5 * i + 1))
        fix = jnp.where(lane8 == 0, a, jnp.where(lane8 == NY - 1, b, 0.0))
        ext = jnp.where(lane8 >= NY - 4, a, jnp.where(lane8 < 4, b, 0.0))
        return fix, ext

    def pack_rows(exts, fixes):
        acc = jnp.zeros((LV, NY), F32)
        for r in range(len(exts)):
            acc = jnp.where((lane8 >= 8 * r) & (lane8 < 8 * r + 8), roll(exts[r], 8 * r + 4), acc)
        for r in range(len(fixes)):
            acc = jnp.where((lane8 >= 40 + 2 * r) & (lane8 < 42 + 2 * r), roll(fixes[r], 41 + 2 * r), acc)
        return acc

    x_lat = lat_exchange(xe.at[0], xe.at[1], xh.at[0], xh.at[1], x_s, x_r, 0)

    zero8 = jnp.zeros((LV, NY), F32)
    for c in args[3:]:
        c.wait()
    for v in range(NV):
        fm[NC + v, M:M + NX] = jnp.transpose(st_ref[v], (1, 0, 2))

    @pl.loop(0, NV, unroll=2)
    def _(v):
        pack_lat(2 * NC + v, [(fm[NC + v, M + x], zero8) for x in range(NX)])

    x_lat()
    c_left = rcopy(xh, xc.at[1], cor_s.at[0], cor_r.at[0], left)
    c_right = rcopy(xh, xc.at[0], cor_s.at[1], cor_r.at[1], right)
    c_left.start()
    c_right.start()
    rows_left[1].start()
    rows_right[1].start()
    q_copies = [
        rcopy(fm.at[NC:NF, M:M + 4], fm.at[NC:NF, M + NX:M + NX + 4], q_s.at[0], q_r.at[0], left),
        rcopy(fm.at[NC:NF, M + NX - 4:M + NX], fm.at[NC:NF, 0:4], q_s.at[1], q_r.at[1], right)]
    for c in q_copies:
        c.start()

    def inject(corners):
        xpos = lanes((CH, NY)) % NX
        kinds = []
        for side in range(2):
            b = 2 * side
            own = xh[side].astype(F32)
            t0, t2 = roll(own, 1), roll(own, -1)
            if corners:
                t0 = jnp.where(xpos == 0, roll(xc[0, side].astype(F32), -(NX - 1)), t0)
                t2 = jnp.where(xpos == NX - 1, roll(xc[1, side].astype(F32), NX - 1), t2)
            taps = jnp.concatenate([t0.astype(BF16), xh[side], t2.astype(BF16)], axis=0)
            e = jnp.dot(lhs1[0, b * CH:(b + 1) * CH, 0:3 * CH], taps, preferred_element_type=F32)
            e_hi = e.astype(BF16).astype(F32)
            kinds += [e_hi, e - e_hi]
        group = lanes((CH, NY)) // 32
        for lp in range(LV // 2):
            inj = jnp.zeros((CH, NY), F32)
            for kind in range(4):
                inj = jnp.where(group == kind, roll(kinds[kind], 32 * kind - 32 * lp), inj)
            lhs1[lp, CH:2 * CH, 3 * CH:] = inj.astype(BF16)
            if not corners:
                lhs1[lp, 0:CH, 3 * CH:] = jnp.zeros((CH, NY), BF16)
                lhs1[lp, 2 * CH:, 3 * CH:] = jnp.zeros((CH, NY), BF16)

    inject(False)

    q_lat = send_lat(2 * NC, NP, 4)

    lane1 = lanes((CH, NY))

    def conv1(lp, x):
        rhs = jnp.concatenate(
            [xt[2 * lp + h, pl.ds(x, 3)].reshape(3 * CH, NY) for h in range(2)], axis=1)
        rhs = jnp.concatenate([rhs, oh[x]], axis=0)
        s = jnp.dot(lhs1[lp], rhs, preferred_element_type=F32)
        for h in range(2):
            c = slice(h * NY, (h + 1) * NY)
            pre = s[CH:2 * CH, c] + bias[...]
            pre = pre + jnp.where(lane1 == 0, 0.0, roll(s[0:CH, c], 1))
            pre = pre + jnp.where(lane1 == NY - 1, 0.0, roll(s[2 * CH:, c], -1))
            half_pre = 0.5 * pre
            ht[2 * lp + h, x + 1] = (half_pre + half_pre * jnp.tanh(half_pre)).astype(BF16)

    lane64 = lanes((64, NY))

    def conv2(lp, j):
        rhs = jnp.concatenate(
            [ht[2 * lp + h, 2 * j:2 * j + 2].reshape(2 * CH, NY) for h in range(2)], axis=1)
        s = jnp.dot(lhs2[...], rhs, preferred_element_type=F32)
        out = []
        for h in range(2):
            c = slice(h * NY, (h + 1) * NY)
            up = roll(s[0:64, c], 1)
            dn = roll(s[128:192, c], -1)
            main = s[64:128, c] + jnp.where(lane64 == 0, 0.0, up) + jnp.where(lane64 == NY - 1, 0.0, dn)
            edge = jnp.where(lane64 == 0, up, 0.0) + jnp.where(lane64 == NY - 1, dn, 0.0)
            out.append((main, edge))
        return out

    def put(lp, row, parts, more=False):
        for h in range(2):
            at = pl.ds(row * (NC * LV) + 2 * lp + h, NC, stride=LV)
            for k, ref in enumerate((pm, pe)):
                t = None
                for pair, off in parts:
                    piece = pair[h][k][off * 16:off * 16 + NC]
                    t = piece if t is None else t + piece
                ref[at, :] = ref[at, :] + t if more else t

    def cell(row, f):
        at = pl.ds(pl.multiple_of((row * NC + f) * LV, LV), LV)
        return pm[at, :], pe[at, :]

    @pl.loop(0, LV)
    def _(i):
        lp, g = i // 2, i % 2
        for u in range(4):
            conv1(lp, 1 + 10 * g + u)

    for c in (c_left, c_right, *rows_left, *rows_right):
        c.wait()
    inject(True)

    @pl.loop(0, LV // 4)
    def _(i):
        for u in range(2):
            conv1(2 * i + u, 0)
            conv1(2 * i + u, NX - 1)

    q_lat()

    @pl.loop(0, NV, unroll=2)
    def _(v):
        exts = []
        for x in range(NX):
            _, ext = from_lat(2 * NC + v, x)
            fe[NC + v, M + x] = ext
            exts.append(ext)
        epk[0, NC + v] = pack_rows(exts[:4], [])
        epk[1, NC + v] = pack_rows(exts[-4:], [])

    q_edges = [
        rcopy(epk.at[0, NC:NF], epr.at[1, NC:NF], q_s.at[2], q_r.at[2], left),
        rcopy(epk.at[1, NC:NF], epr.at[0, NC:NF], q_s.at[3], q_r.at[3], right)]
    for c in q_edges:
        c.start()

    @pl.loop(0, LV // 2)
    def _(lp):
        p = [conv2(lp, j) for j in range(3)]
        put(lp, 0, [(p[0], 1)])
        for i in range(2):
            put(lp, 1 + i, [(p[0], 2 + i), (p[1], i)])
            put(lp, 3 + i, [(p[1], 2 + i), (p[2], i)])
            put(lp, 5 + i, [(p[2], 2 + i)])
        p = [conv2(lp, j) for j in range(6, 9)]
        for i in range(2):
            put(lp, 11 + i, [(p[0], i)])
            put(lp, 13 + i, [(p[0], 2 + i), (p[1], i)])
            put(lp, 15 + i, [(p[1], 2 + i), (p[2], i)])
        put(lp, 17, [(p[2], 2)])

    def rows_part(k, lo_, hi_):
        at, to = pl.ds(lo_ * NC * LV, (hi_ - lo_) * NC * LV), NR - 5
        far = pl.ds((to + lo_) * NC * LV, (hi_ - lo_) * NC * LV)
        return [rcopy(pm.at[at], rowr.at[1, at], lon_s.at[k], lon_r.at[k], left),
                rcopy(pm.at[far], rowr.at[0, at], lon_s.at[k + 1], lon_r.at[k + 1], right)]

    first_rows = rows_part(0, 0, 2)
    last_rows = rows_part(4, 2, 5)
    for c in first_rows:
        c.start()

    outer = [0, 1, 2, 3, 4, NR - 5, NR - 4, NR - 3, NR - 2, NR - 1]
    inner = list(range(5, NR - 5))

    @pl.loop(0, NC, unroll=2)
    def _(f):
        pack_lat(f, [cell(r, f) for r in outer])

    outer_lat = send_lat(0, NC, 0)

    @pl.loop(0, LV // 2)
    def _(lp):
        for x in range(5, NX - 7):
            conv1(lp, x)

    outer_lat()
    for c in last_rows:
        c.start()

    @pl.loop(0, LV // 4)
    def _(i):
        for u in range(2):
            for x in range(NX - 7, NX - 5):
                conv1(2 * i + u, x)

    def take(slot, i, row, f):
        m, e = cell(row, f)
        fix, ext = from_lat(slot, i)
        fm[f, M - 1 + row] = m + fix
        fe[f, M - 1 + row] = e + ext
        return fix, e + ext

    @pl.loop(0, NC, unroll=2)
    def _(f):
        got = [take(f, i, r, f) for i, r in enumerate(outer)]
        epk[0, f] = pack_rows([g[1] for g in got[:5]], [g[0] for g in got[:5]])
        epk[1, f] = pack_rows([g[1] for g in got[5:]], [g[0] for g in got[5:]])

    e_left = rcopy(epk.at[0, 0:NC], epr.at[1, 0:NC], lon_s.at[2], lon_r.at[2], left)
    e_right = rcopy(epk.at[1, 0:NC], epr.at[0, 0:NC], lon_s.at[3], lon_r.at[3], right)
    e_left.start()
    e_right.start()

    @pl.loop(0, LV // 2)
    def _(lp):
        p = [conv2(lp, j) for j in range(3, 6)]
        for i in range(2):
            put(lp, 5 + i, [(p[0], i)], True)
            put(lp, 7 + i, [(p[0], 2 + i), (p[1], i)])
            put(lp, 9 + i, [(p[1], 2 + i), (p[2], i)])
            put(lp, 11 + i, [(p[2], 2 + i)], True)

    @pl.loop(0, NC, unroll=2)
    def _(f):
        pack_lat(NC + f, [cell(r, f) for r in inner])

    inner_lat = send_lat(NC, 2 * NC, 2)

    for c in (*q_copies, *q_edges):
        c.wait()

    def ext_lanes(t):
        return jnp.where((lane8 < 4) | (lane8 >= NY - 4), t, 0.0)

    @pl.loop(NC, NF)
    def _(f):
        for side in range(2):
            t = epr[side, f]
            for r in range(4):
                fe[f, (0 if side == 0 else M + NX) + r] = ext_lanes(roll(t, -(8 * r + 4)))

    inner_lat()

    @pl.loop(0, NC, unroll=2)
    def _(f):
        for i, r in enumerate(inner):
            take(NC + f, i, r, f)

    for c in (*first_rows, *last_rows, e_left, e_right):
        c.wait()

    @pl.loop(0, NC, unroll=2)
    def _(f):
        for side in range(2):
            t = epr[side, f]
            for r in range(5):
                x = (r if side == 0 else M + NX - 1 + r)
                fix = jnp.where((lane8 == 0) | (lane8 == NY - 1), roll(t, -(41 + 2 * r)), 0.0)
                got = rowr[side, pl.ds(pl.multiple_of((r * NC + f) * LV, LV), LV), :] + fix
                ext = ext_lanes(roll(t, -(8 * r + 4)))
                if x < M - 1 or x > M + NX:
                    fm[f, x] = got
                    fe[f, x] = ext
                else:
                    fm[f, x] = fm[f, x] + got
                    fe[f, x] = fe[f, x] + ext

    cos_m = tab_ref[lat, 0, :, 0:NY]
    cos_e = tab_ref[lat, 0, :, NY:]
    cap_m = tab_ref[lat, 1, :, 0:NY]
    cap_e = tab_ref[lat, 1, :, NY:]
    met_m = 1.0 / cos_m
    met_e = 1.0 / cos_e

    def shift(m, e, step):
        sh = 1 if step < 0 else -1
        edge = 0 if step < 0 else NY - 1
        rm, re = roll(m, sh), roll(e, sh)
        at = lanes(m.shape) == edge
        return jnp.where(at, re, rm), jnp.where(at, rm, re)

    @pl.loop(0, NV)
    def _(v):
        bu = b2_ref[2 * v]
        bv = b2_ref[2 * v + 1]
        um = cap_m * jnp.tanh(fm[2 * v] + bu)
        ue = cap_e * jnp.tanh(fe[2 * v] + bu)
        vm = cap_m * jnp.tanh(fm[2 * v + 1] + bv)
        ve = cap_e * jnp.tanh(fe[2 * v + 1] + bv)
        vel_ref[2 * v] = um[M:M + NX]
        vel_ref[2 * v + 1] = vm[M:M + NX]
        i = slice(1, EX - 1)
        fn_m, fn_e = shift(vm[i] * cos_m, ve[i] * cos_e, 1)
        fs_m, fs_e = shift(vm[i] * cos_m, ve[i] * cos_e, -1)

        def coef(u, vv, met, fn, fs):
            div = met * ((u[2:] - u[:-2]) * 0.5 + (fn - fs) * 0.5)
            up, un = met * jnp.maximum(u[i], 0.0), met * jnp.minimum(u[i], 0.0)
            vp, vn = jnp.maximum(vv[i], 0.0), jnp.minimum(vv[i], 0.0)
            return (un - up) + (vn - vp) - div, up, un, vp, vn

        cm = coef(um, vm, met_m, fn_m, fs_m)
        ce = coef(ue, ve, met_e, fn_e, fs_e)

        def rate(qm, qe, k):
            n = EX - 2 * k
            nm, ne = shift(qm[1:-1], qe[1:-1], 1)
            sm, se = shift(qm[1:-1], qe[1:-1], -1)

            def one(q, c, qn, qs):
                c0, up, un, vp, vn = (t[k - 1:k - 1 + n] for t in c)
                return c0 * q[1:-1] + up * q[:-2] - un * q[2:] + vp * qs - vn * qn
            return one(qm, cm, nm, sm), one(qe, ce, ne, se)

        qm = fm[NC + v]
        qe = fe[NC + v]
        r1m, r1e = rate(qm, qe, 1)
        tot = r1m[3:3 + NX]
        r2m, r2e = rate(qm[1:-1] + 0.25 * r1m, qe[1:-1] + 0.25 * r1e, 2)
        tot = tot + 2.0 * r2m[2:2 + NX]
        r3m, r3e = rate(qm[2:-2] + 0.25 * r2m, qe[2:-2] + 0.25 * r2e, 3)
        tot = tot + 2.0 * r3m[1:1 + NX]
        r4m, _ = rate(qm[3:-3] + 0.5 * r3m, qe[3:-3] + 0.5 * r3e, 4)
        tend_ref[v] = (tot + r4m) * (1.0 / 6.0)


def solution(mesh):
    n_lon, n_lat = mesh.shape["lon"], mesh.shape["lat"]
    tables = lat_tables(n_lat)

    def body(hidden_in, w1, b1, w2, b2, state):
        vmem = pl.BlockSpec(memory_space=pltpu.VMEM)
        hbm = pl.BlockSpec(memory_space=pltpu.HBM)

        def keep(array):
            return pltpu.with_memory_space_constraint(array, pltpu.HBM)
        dma = pltpu.SemaphoreType.DMA
        vel, tend = pl.pallas_call(
            functools.partial(kernel, n_lon, n_lat),
            out_shape=(jax.ShapeDtypeStruct((NC, NX, LV, NY), F32),
                       jax.ShapeDtypeStruct((NV, NX, LV, NY), F32)),
            in_specs=[hbm, hbm, hbm, hbm, pl.BlockSpec(memory_space=pltpu.SMEM), hbm, hbm],
            out_specs=(vmem, vmem),
            scratch_shapes=[
                pltpu.VMEM(w1.shape, BF16),
                pltpu.VMEM((1, CH), F32),
                pltpu.VMEM((3, 3, NC, CH), BF16),
                pltpu.VMEM((NV, LV, NX, NY), F32),
                pltpu.VMEM(tables.shape, F32),
                dma((5,)),
                pltpu.VMEM((LV, CH, NX, NY), BF16),
                pltpu.VMEM((LV, NX + 2, CH, NY), BF16),
                pltpu.VMEM((LV, NX + 2, CH, NY), BF16),
                pltpu.VMEM((LV // 2, 3 * CH, 4 * CH), BF16),
                pltpu.VMEM((192, 2 * CH), BF16),
                pltpu.VMEM((NX, CH, 2 * NY), BF16),
                pltpu.VMEM((NX, CH, 2 * NY), BF16),
                pltpu.VMEM((CH, NY), F32),
                pltpu.VMEM((2, CH, NY), BF16),
                pltpu.VMEM((2, CH, NY), BF16),
                pltpu.VMEM((2, 2, CH, NY), BF16),
                pltpu.VMEM((NR * NC * LV, NY), F32),
                pltpu.VMEM((NR * NC * LV, NY), F32),
                pltpu.VMEM((NF, EX, LV, NY), F32),
                pltpu.VMEM((NF, EX, LV, NY), F32),
                pltpu.VMEM((2, NP, LV, NY), F32),
                pltpu.VMEM((2, NP, LV, NY), F32),
                pltpu.VMEM((2, 5 * NC * LV, NY), F32),
                pltpu.VMEM((2, NF, LV, NY), F32),
                pltpu.VMEM((2, NF, LV, NY), F32),
                dma((LV,)), dma((2,)), dma((2,)), dma((4,)), dma((4,)), dma((2,)), dma((2,)),
                dma((6,)), dma((6,)), dma((6,)), dma((6,)), dma((4,)), dma((4,)),
            ],
            compiler_params=pltpu.CompilerParams(
                collective_id=0, has_side_effects=True, vmem_limit_bytes=44 * 1024 * 1024),
        )(keep(hidden_in), keep(w1), keep(b1.reshape(1, CH)), keep(jnp.transpose(w2, (0, 1, 3, 2))), keep(b2),
          keep(state), keep(jnp.asarray(tables)))
        return jnp.transpose(vel, (0, 2, 1, 3)), jnp.transpose(tend, (0, 2, 1, 3))

    spread = P(None, None, "lon", "lat")
    return jax.shard_map(
        body, mesh=mesh, in_specs=(spread, P(), P(), P(), P(), spread),
        out_specs=(spread, spread), check_vma=False)
```

```python
import functools
import math

import jax
import jax.numpy as jnp
import numpy as np
from jax import lax
from jax.experimental import pallas as pl
from jax.experimental.pallas import tpu as pltpu
from jax.sharding import PartitionSpec as P

MESH = pl.DeviceIdType.MESH
F32 = jnp.float32
BF16 = jnp.bfloat16
TIME_STEP = 0.5
SPEED_CAP = 0.6
COS_FLOOR = 0.5
NV = 6
NC = 12
NF = 18
LV = 8
NX = 16
NY = 128
CH = 128
M = 4
EX = NX + 2 * M
NR = NX + 2
NP = 2 * NC + NV
HALF = LV // 2


def lat_tables(n_lat_dev):
    n_lat = n_lat_dev * NY
    out = np.zeros((n_lat_dev, 2, LV, 2 * NY), np.float32)
    for d in range(n_lat_dev):
        lane = np.arange(2 * NY)
        y = np.where(lane < NY + NY // 2, lane, lane - 2 * NY) + d * NY
        phi = (y + 0.5) * (math.pi / n_lat) - 0.5 * math.pi
        inside = ((y >= 0) & (y < n_lat)).astype(np.float32)
        out[d, 0] = np.maximum(np.cos(phi), COS_FLOOR)[None]
        out[d, 1] = (SPEED_CAP * inside)[None]
    return out


def lanes(shape):
    return lax.broadcasted_iota(jnp.int32, shape, len(shape) - 1)


def roll(v, s):
    s = s % NY
    return v if s == 0 else pltpu.roll(v, s, v.ndim - 1)


def kernel(n_lon, n_lat, x_hbm, w1_hbm, b1_hbm, w2_hbm, b2_ref, st_hbm, tab_hbm,
           vel_ref, tend_ref,
           w1_ref, b1_ref, w2_ref, st_ref, tab_ref, arg_sem, xin, xt, ht, lhs1, lhs2, oh, ohe, bias, xe, xh, xs, xc, pm, pe, fm, fe, pk, pr, rowr, epk, epr,
           in_sem, x_s, x_r, row_s, row_r, cor_s, cor_r, lat_s, lat_r, lon_s, lon_r, q_s, q_r):
    lon = lax.axis_index("lon")
    lat = lax.axis_index("lat")
    left = (lax.rem(lon + n_lon - 1, n_lon), lat)
    right = (lax.rem(lon + 1, n_lon), lat)
    south = (lon, lat - 1)
    north = (lon, lat + 1)
    has_s = lat > 0
    has_n = lat < n_lat - 1

    for side, has in ((0, has_s), (1, has_n)):
        @pl.when(jnp.logical_not(has))
        def _():
            xh[side] = jnp.zeros((CH, NY), BF16)
            pr[side] = jnp.zeros((NP, LV, NY), F32)

    barrier = pltpu.get_barrier_semaphore()
    for dev in (left, right):
        pl.semaphore_signal(barrier, inc=1, device_id=dev, device_id_type=MESH)

    @pl.when(has_s)
    def _():
        pl.semaphore_signal(barrier, inc=1, device_id=south, device_id_type=MESH)

    @pl.when(has_n)
    def _():
        pl.semaphore_signal(barrier, inc=1, device_id=north, device_id_type=MESH)

    loads = [pltpu.make_async_copy(x_hbm.at[l], xin.at[l], in_sem.at[l]) for l in range(LV)]
    args = [pltpu.make_async_copy(src, dst, arg_sem.at[i]) for i, (src, dst) in enumerate(
        ((w1_hbm, w1_ref), (w2_hbm, w2_ref), (b1_hbm, b1_ref), (st_hbm, st_ref), (tab_hbm, tab_ref)))]
    for c in (*args[:3], *loads, *args[3:]):
        c.start()

    k_id = lax.broadcasted_iota(jnp.int32, (CH, 2 * NY), 0)
    lane2 = lanes((CH, 2 * NY))
    half = (k_id // 16) % 2
    target = half * NY + jnp.where(k_id < 64, 0, NY - 1)
    hit = lane2 == target

    @pl.loop(0, NX)
    def _(x):
        oh[x] = jnp.where(hit & (k_id % 16 == x), 1.0, 0.0).astype(BF16)
        want_hi = (k_id == NY - 1) & (lane2 == x)
        want_lo = (k_id == 0) & (lane2 == NY + x)
        ohe[x] = jnp.where(want_hi | want_lo, 1.0, 0.0).astype(BF16)

    for c in args[:3]:
        c.wait()
    for b in range(3):
        for a in range(3):
            lhs1[0, b * CH:(b + 1) * CH, a * CH:(a + 1) * CH] = jnp.transpose(w1_ref[a, b], (1, 0))
    for lp in range(1, LV // 2):
        lhs1[lp, :, 0:3 * CH] = lhs1[0, :, 0:3 * CH]
    lhs2[...] = jnp.zeros_like(lhs2)
    for b in range(3):
        for off in range(4):
            for r in range(2):
                a = r - off + 2
                if 0 <= a <= 2:
                    base = b * 64 + off * 16
                    lhs2[base:base + NC, r * CH:(r + 1) * CH] = w2_ref[a, b]
    bias[...] = jnp.transpose(jnp.broadcast_to(b1_ref[...], (CH, CH)), (1, 0))
    ht[:, 0] = jnp.zeros((LV, CH, NY), BF16)
    ht[:, NX + 1] = jnp.zeros((LV, CH, NY), BF16)

    def rcopy(src, dst, ss, rs_, dev):
        return pltpu.make_async_remote_copy(src_ref=src, dst_ref=dst, send_sem=ss, recv_sem=rs_,
                                            device_id=dev, device_id_type=MESH)

    hi = jnp.zeros((CH, NY), F32)
    lo = jnp.zeros((CH, NY), F32)
    rows_left, rows_right = [], []
    for l in range(LV):
        loads[l].wait()
        xt[l, 1:NX + 1] = jnp.transpose(xin[l], (1, 0, 2))
        if l % 2 == 1:
            row = jnp.concatenate(
                [jnp.concatenate([xt[l - 1 + h, 1 + x] for x in range(NX)], axis=1) for h in range(2)], axis=0)
            res = jnp.dot(row, ohe[...].reshape(NX * NY, 2 * NY), preferred_element_type=F32)
            for h in range(2):
                hi = hi + roll(res[h * CH:(h + 1) * CH, :NY], 16 * (l - 1 + h))
                lo = lo + roll(res[h * CH:(h + 1) * CH, NY:], 16 * (l - 1 + h))
        if l == HALF - 1:
            pl.semaphore_wait(barrier, 2 + has_s.astype(jnp.int32) + has_n.astype(jnp.int32))
        if (l + 1) % HALF == 0:
            g = l // HALF
            part = slice(g * HALF, (g + 1) * HALF)
            rows_left.append(rcopy(xt.at[part, 1], xt.at[part, NX + 1], row_s.at[g], row_r.at[g], left))
            rows_right.append(rcopy(xt.at[part, NX], xt.at[part, 0], row_s.at[2 + g], row_r.at[2 + g], right))
            if g == 0:
                rows_left[0].start()
                rows_right[0].start()
    xe[0] = hi.astype(BF16)
    xe[1] = lo.astype(BF16)

    def lat_exchange(src_n, src_s, dst_from_s, dst_from_n, sems, semr, at):
        to_n = rcopy(src_n, dst_from_s, sems.at[at], semr.at[at], north)
        to_s = rcopy(src_s, dst_from_n, sems.at[at + 1], semr.at[at + 1], south)

        @pl.when(has_n)
        def _():
            to_n.start()

        @pl.when(has_s)
        def _():
            to_s.start()

        def finish():
            @pl.when(has_s)
            def _():
                to_n.wait_recv()
                to_s.wait_send()

            @pl.when(has_n)
            def _():
                to_s.wait_recv()
                to_n.wait_send()
        return finish

    lane8 = lanes((LV, NY))

    def pack_lat(slot, cells):
        to_n = jnp.zeros((LV, NY), F32)
        to_s = jnp.zeros((LV, NY), F32)
        for i, (m, e) in enumerate(cells):
            mine = (lane8 >= 5 * i) & (lane8 < 5 * i + 5)
            to_n = jnp.where(mine, roll(jnp.where(lane8 == 0, e, m), 5 * i + 4), to_n)
            to_s = jnp.where(mine, roll(jnp.where(lane8 == NY - 1, e, m), 5 * i + 1), to_s)
        pk[0, slot] = to_n
        pk[1, slot] = to_s

    def send_lat(lo_, hi_, at):
        return lat_exchange(pk.at[0, lo_:hi_], pk.at[1, lo_:hi_], pr.at[0, lo_:hi_], pr.at[1, lo_:hi_],
                            lat_s, lat_r, at)

    def from_lat(slot, i):
        a = roll(pr[0, slot], -(5 * i + 4))
        b = roll(pr[1, slot], -(5 * i + 1))
        fix = jnp.where(lane8 == 0, a, jnp.where(lane8 == NY - 1, b, 0.0))
        ext = jnp.where(lane8 >= NY - 4, a, jnp.where(lane8 < 4, b, 0.0))
        return fix, ext

    def pack_rows(exts, fixes):
        acc = jnp.zeros((LV, NY), F32)
        for r in range(len(exts)):
            acc = jnp.where((lane8 >= 8 * r) & (lane8 < 8 * r + 8), roll(exts[r], 8 * r + 4), acc)
        for r in range(len(fixes)):
            acc = jnp.where((lane8 >= 40 + 2 * r) & (lane8 < 42 + 2 * r), roll(fixes[r], 41 + 2 * r), acc)
        return acc

    x_lat = lat_exchange(xe.at[0], xe.at[1], xh.at[0], xh.at[1], x_s, x_r, 0)

    zero8 = jnp.zeros((LV, NY), F32)
    for c in args[3:]:
        c.wait()
    for v in range(NV):
        fm[NC + v, M:M + NX] = jnp.transpose(st_ref[v], (1, 0, 2))

    @pl.loop(0, NV, unroll=2)
    def _(v):
        pack_lat(2 * NC + v, [(fm[NC + v, M + x], zero8) for x in range(NX)])

    x_lat()
    xpos = lanes((CH, NY)) % NX
    h0, h1 = xh[0].astype(F32), xh[1].astype(F32)
    xs[0] = jnp.where(xpos == 0, h0, roll(h1, 1)).astype(BF16)
    xs[1] = jnp.where(xpos == NX - 1, h0, roll(h1, -1)).astype(BF16)
    c_left = rcopy(xs.at[0], xc.at[1], cor_s.at[0], cor_r.at[0], left)
    c_right = rcopy(xs.at[1], xc.at[0], cor_s.at[1], cor_r.at[1], right)
    c_left.start()
    c_right.start()
    rows_left[1].start()
    rows_right[1].start()
    q_copies = [
        rcopy(fm.at[NC:NF, M:M + 4], fm.at[NC:NF, M + NX:M + NX + 4], q_s.at[0], q_r.at[0], left),
        rcopy(fm.at[NC:NF, M + NX - 4:M + NX], fm.at[NC:NF, 0:4], q_s.at[1], q_r.at[1], right)]
    for c in q_copies:
        c.start()

    def inject(corners):
        kinds = []
        for side in range(2):
            b = 2 * side
            own = xh[side].astype(F32)
            t0, t2 = roll(own, 1), roll(own, -1)
            if corners:
                t0 = jnp.where(xpos == 0, roll(xc[0].astype(F32), side - (NX - 1)), t0)
                t2 = jnp.where(xpos == NX - 1, roll(xc[1].astype(F32), NX - 1 - side), t2)
            taps = jnp.concatenate([t0.astype(BF16), xh[side], t2.astype(BF16)], axis=0)
            e = jnp.dot(lhs1[0, b * CH:(b + 1) * CH, 0:3 * CH], taps, preferred_element_type=F32)
            e_hi = e.astype(BF16).astype(F32)
            kinds += [e_hi, e - e_hi]
        group = lanes((CH, NY)) // 32
        for lp in range(LV // 2):
            inj = jnp.zeros((CH, NY), F32)
            for kind in range(4):
                inj = jnp.where(group == kind, roll(kinds[kind], 32 * kind - 32 * lp), inj)
            lhs1[lp, CH:2 * CH, 3 * CH:] = inj.astype(BF16)
            if not corners:
                lhs1[lp, 0:CH, 3 * CH:] = jnp.zeros((CH, NY), BF16)
                lhs1[lp, 2 * CH:, 3 * CH:] = jnp.zeros((CH, NY), BF16)

    inject(False)

    q_lat = send_lat(2 * NC, NP, 4)

    lane1 = lanes((CH, NY))

    def conv1(lp, x):
        rhs = jnp.concatenate(
            [xt[2 * lp + h, pl.ds(x, 3)].reshape(3 * CH, NY) for h in range(2)], axis=1)
        rhs = jnp.concatenate([rhs, oh[x]], axis=0)
        s = jnp.dot(lhs1[lp], rhs, preferred_element_type=F32)
        for h in range(2):
            c = slice(h * NY, (h + 1) * NY)
            pre = s[CH:2 * CH, c] + bias[...]
            pre = pre + jnp.where(lane1 == 0, 0.0, roll(s[0:CH, c], 1))
            pre = pre + jnp.where(lane1 == NY - 1, 0.0, roll(s[2 * CH:, c], -1))
            half_pre = 0.5 * pre
            ht[2 * lp + h, x + 1] = (half_pre + half_pre * jnp.tanh(half_pre)).astype(BF16)

    lane64 = lanes((64, NY))

    def conv2(lp, j):
        rhs = jnp.concatenate(
            [ht[2 * lp + h, 2 * j:2 * j + 2].reshape(2 * CH, NY) for h in range(2)], axis=1)
        s = jnp.dot(lhs2[...], rhs, preferred_element_type=F32)
        out = []
        for h in range(2):
            c = slice(h * NY, (h + 1) * NY)
            up = roll(s[0:64, c], 1)
            dn = roll(s[128:192, c], -1)
            main = s[64:128, c] + jnp.where(lane64 == 0, 0.0, up) + jnp.where(lane64 == NY - 1, 0.0, dn)
            edge = jnp.where(lane64 == 0, up, 0.0) + jnp.where(lane64 == NY - 1, dn, 0.0)
            out.append((main, edge))
        return out

    def put(lp, row, parts, more=False):
        for h in range(2):
            at = pl.ds(row * (NC * LV) + 2 * lp + h, NC, stride=LV)
            for k, ref in enumerate((pm, pe)):
                t = None
                for pair, off in parts:
                    piece = pair[h][k][off * 16:off * 16 + NC]
                    t = piece if t is None else t + piece
                ref[at, :] = ref[at, :] + t if more else t

    def cell(row, f):
        at = pl.ds(pl.multiple_of((row * NC + f) * LV, LV), LV)
        return pm[at, :], pe[at, :]

    @pl.loop(0, LV)
    def _(i):
        lp, g = i // 2, i % 2
        for u in range(4):
            conv1(lp, 1 + 10 * g + u)

    for c in (c_left, c_right, *rows_left, *rows_right):
        c.wait()
    inject(True)

    @pl.loop(0, LV // 4)
    def _(i):
        for u in range(2):
            conv1(2 * i + u, 0)
            conv1(2 * i + u, NX - 1)

    q_lat()

    @pl.loop(0, NV, unroll=2)
    def _(v):
        exts = []
        for x in range(NX):
            _, ext = from_lat(2 * NC + v, x)
            fe[NC + v, M + x] = ext
            exts.append(ext)
        epk[0, NC + v] = pack_rows(exts[:4], [])
        epk[1, NC + v] = pack_rows(exts[-4:], [])

    q_edges = [
        rcopy(epk.at[0, NC:NF], epr.at[1, NC:NF], q_s.at[2], q_r.at[2], left),
        rcopy(epk.at[1, NC:NF], epr.at[0, NC:NF], q_s.at[3], q_r.at[3], right)]
    for c in q_edges:
        c.start()

    @pl.loop(0, LV // 2)
    def _(lp):
        p = [conv2(lp, j) for j in range(3)]
        put(lp, 0, [(p[0], 1)])
        for i in range(2):
            put(lp, 1 + i, [(p[0], 2 + i), (p[1], i)])
            put(lp, 3 + i, [(p[1], 2 + i), (p[2], i)])
            put(lp, 5 + i, [(p[2], 2 + i)])
        p = [conv2(lp, j) for j in range(6, 9)]
        for i in range(2):
            put(lp, 11 + i, [(p[0], i)])
            put(lp, 13 + i, [(p[0], 2 + i), (p[1], i)])
            put(lp, 15 + i, [(p[1], 2 + i), (p[2], i)])
        put(lp, 17, [(p[2], 2)])

    def rows_part(k, lo_, hi_):
        at, to = pl.ds(lo_ * NC * LV, (hi_ - lo_) * NC * LV), NR - 5
        far = pl.ds((to + lo_) * NC * LV, (hi_ - lo_) * NC * LV)
        return [rcopy(pm.at[at], rowr.at[1, at], lon_s.at[k], lon_r.at[k], left),
                rcopy(pm.at[far], rowr.at[0, at], lon_s.at[k + 1], lon_r.at[k + 1], right)]

    first_rows = rows_part(0, 0, 2)
    last_rows = rows_part(4, 2, 5)
    for c in first_rows:
        c.start()

    outer = [0, 1, 2, 3, 4, NR - 5, NR - 4, NR - 3, NR - 2, NR - 1]
    inner = list(range(5, NR - 5))

    @pl.loop(0, NC, unroll=2)
    def _(f):
        pack_lat(f, [cell(r, f) for r in outer])

    outer_lat = send_lat(0, NC, 0)

    @pl.loop(0, LV // 2)
    def _(lp):
        for x in range(5, NX - 7):
            conv1(lp, x)

    outer_lat()
    for c in last_rows:
        c.start()

    @pl.loop(0, LV // 4)
    def _(i):
        for u in range(2):
            for x in range(NX - 7, NX - 5):
                conv1(2 * i + u, x)

    def take(slot, i, row, f):
        m, e = cell(row, f)
        fix, ext = from_lat(slot, i)
        fm[f, M - 1 + row] = m + fix
        fe[f, M - 1 + row] = e + ext
        return fix, e + ext

    @pl.loop(0, NC, unroll=2)
    def _(f):
        got = [take(f, i, r, f) for i, r in enumerate(outer)]
        epk[0, f] = pack_rows([g[1] for g in got[:5]], [g[0] for g in got[:5]])
        epk[1, f] = pack_rows([g[1] for g in got[5:]], [g[0] for g in got[5:]])

    e_left = rcopy(epk.at[0, 0:NC], epr.at[1, 0:NC], lon_s.at[2], lon_r.at[2], left)
    e_right = rcopy(epk.at[1, 0:NC], epr.at[0, 0:NC], lon_s.at[3], lon_r.at[3], right)
    e_left.start()
    e_right.start()

    @pl.loop(0, LV // 2)
    def _(lp):
        p = [conv2(lp, j) for j in range(3, 6)]
        for i in range(2):
            put(lp, 5 + i, [(p[0], i)], True)
            put(lp, 7 + i, [(p[0], 2 + i), (p[1], i)])
            put(lp, 9 + i, [(p[1], 2 + i), (p[2], i)])
            put(lp, 11 + i, [(p[2], 2 + i)], True)

    @pl.loop(0, NC, unroll=2)
    def _(f):
        pack_lat(NC + f, [cell(r, f) for r in inner])

    inner_lat = send_lat(NC, 2 * NC, 2)

    for c in (*q_copies, *q_edges):
        c.wait()

    def ext_lanes(t):
        return jnp.where((lane8 < 4) | (lane8 >= NY - 4), t, 0.0)

    @pl.loop(NC, NF)
    def _(f):
        for side in range(2):
            t = epr[side, f]
            for r in range(4):
                fe[f, (0 if side == 0 else M + NX) + r] = ext_lanes(roll(t, -(8 * r + 4)))

    inner_lat()

    @pl.loop(0, NC, unroll=2)
    def _(f):
        for i, r in enumerate(inner):
            take(NC + f, i, r, f)

    for c in (*first_rows, *last_rows, e_left, e_right):
        c.wait()

    @pl.loop(0, NC, unroll=2)
    def _(f):
        for side in range(2):
            t = epr[side, f]
            for r in range(5):
                x = (r if side == 0 else M + NX - 1 + r)
                fix = jnp.where((lane8 == 0) | (lane8 == NY - 1), roll(t, -(41 + 2 * r)), 0.0)
                got = rowr[side, pl.ds(pl.multiple_of((r * NC + f) * LV, LV), LV), :] + fix
                ext = ext_lanes(roll(t, -(8 * r + 4)))
                if x < M - 1 or x > M + NX:
                    fm[f, x] = got
                    fe[f, x] = ext
                else:
                    fm[f, x] = fm[f, x] + got
                    fe[f, x] = fe[f, x] + ext

    cos_m = tab_ref[lat, 0, :, 0:NY]
    cos_e = tab_ref[lat, 0, :, NY:]
    cap_m = tab_ref[lat, 1, :, 0:NY]
    cap_e = tab_ref[lat, 1, :, NY:]
    met_m = 1.0 / cos_m
    met_e = 1.0 / cos_e

    def shift(m, e, step):
        sh = 1 if step < 0 else -1
        edge = 0 if step < 0 else NY - 1
        rm, re = roll(m, sh), roll(e, sh)
        at = lanes(m.shape) == edge
        return jnp.where(at, re, rm), jnp.where(at, rm, re)

    @pl.loop(0, NV)
    def _(v):
        bu = b2_ref[2 * v]
        bv = b2_ref[2 * v + 1]
        um = cap_m * jnp.tanh(fm[2 * v] + bu)
        ue = cap_e * jnp.tanh(fe[2 * v] + bu)
        vm = cap_m * jnp.tanh(fm[2 * v + 1] + bv)
        ve = cap_e * jnp.tanh(fe[2 * v + 1] + bv)
        vel_ref[2 * v] = um[M:M + NX]
        vel_ref[2 * v + 1] = vm[M:M + NX]
        i = slice(1, EX - 1)
        fn_m, fn_e = shift(vm[i] * cos_m, ve[i] * cos_e, 1)
        fs_m, fs_e = shift(vm[i] * cos_m, ve[i] * cos_e, -1)

        def coef(u, vv, met, fn, fs):
            div = met * ((u[2:] - u[:-2]) * 0.5 + (fn - fs) * 0.5)
            up, un = met * jnp.maximum(u[i], 0.0), met * jnp.minimum(u[i], 0.0)
            vp, vn = jnp.maximum(vv[i], 0.0), jnp.minimum(vv[i], 0.0)
            return (un - up) + (vn - vp) - div, up, un, vp, vn

        cm = coef(um, vm, met_m, fn_m, fs_m)
        ce = coef(ue, ve, met_e, fn_e, fs_e)

        def rate(qm, qe, k):
            n = EX - 2 * k
            nm, ne = shift(qm[1:-1], qe[1:-1], 1)
            sm, se = shift(qm[1:-1], qe[1:-1], -1)

            def one(q, c, qn, qs):
                c0, up, un, vp, vn = (t[k - 1:k - 1 + n] for t in c)
                return c0 * q[1:-1] + up * q[:-2] - un * q[2:] + vp * qs - vn * qn
            return one(qm, cm, nm, sm), one(qe, ce, ne, se)

        qm = fm[NC + v]
        qe = fe[NC + v]
        r1m, r1e = rate(qm, qe, 1)
        tot = r1m[3:3 + NX]
        r2m, r2e = rate(qm[1:-1] + 0.25 * r1m, qe[1:-1] + 0.25 * r1e, 2)
        tot = tot + 2.0 * r2m[2:2 + NX]
        r3m, r3e = rate(qm[2:-2] + 0.25 * r2m, qe[2:-2] + 0.25 * r2e, 3)
        tot = tot + 2.0 * r3m[1:1 + NX]
        r4m, _ = rate(qm[3:-3] + 0.5 * r3m, qe[3:-3] + 0.5 * r3e, 4)
        tend_ref[v] = (tot + r4m) * (1.0 / 6.0)


def solution(mesh):
    n_lon, n_lat = mesh.shape["lon"], mesh.shape["lat"]
    tables = lat_tables(n_lat)

    def body(hidden_in, w1, b1, w2, b2, state):
        vmem = pl.BlockSpec(memory_space=pltpu.VMEM)
        hbm = pl.BlockSpec(memory_space=pltpu.HBM)

        def keep(array):
            return pltpu.with_memory_space_constraint(array, pltpu.HBM)
        dma = pltpu.SemaphoreType.DMA
        vel, tend = pl.pallas_call(
            functools.partial(kernel, n_lon, n_lat),
            out_shape=(jax.ShapeDtypeStruct((NC, NX, LV, NY), F32),
                       jax.ShapeDtypeStruct((NV, NX, LV, NY), F32)),
            in_specs=[hbm, hbm, hbm, hbm, pl.BlockSpec(memory_space=pltpu.SMEM), hbm, hbm],
            out_specs=(vmem, vmem),
            scratch_shapes=[
                pltpu.VMEM(w1.shape, BF16),
                pltpu.VMEM((1, CH), F32),
                pltpu.VMEM((3, 3, NC, CH), BF16),
                pltpu.VMEM((NV, LV, NX, NY), F32),
                pltpu.VMEM(tables.shape, F32),
                dma((5,)),
                pltpu.VMEM((LV, CH, NX, NY), BF16),
                pltpu.VMEM((LV, NX + 2, CH, NY), BF16),
                pltpu.VMEM((LV, NX + 2, CH, NY), BF16),
                pltpu.VMEM((LV // 2, 3 * CH, 4 * CH), BF16),
                pltpu.VMEM((192, 2 * CH), BF16),
                pltpu.VMEM((NX, CH, 2 * NY), BF16),
                pltpu.VMEM((NX, CH, 2 * NY), BF16),
                pltpu.VMEM((CH, NY), F32),
                pltpu.VMEM((2, CH, NY), BF16),
                pltpu.VMEM((2, CH, NY), BF16),
                pltpu.VMEM((2, CH, NY), BF16),
                pltpu.VMEM((2, CH, NY), BF16),
                pltpu.VMEM((NR * NC * LV, NY), F32),
                pltpu.VMEM((NR * NC * LV, NY), F32),
                pltpu.VMEM((NF, EX, LV, NY), F32),
                pltpu.VMEM((NF, EX, LV, NY), F32),
                pltpu.VMEM((2, NP, LV, NY), F32),
                pltpu.VMEM((2, NP, LV, NY), F32),
                pltpu.VMEM((2, 5 * NC * LV, NY), F32),
                pltpu.VMEM((2, NF, LV, NY), F32),
                pltpu.VMEM((2, NF, LV, NY), F32),
                dma((LV,)), dma((2,)), dma((2,)), dma((4,)), dma((4,)), dma((2,)), dma((2,)),
                dma((6,)), dma((6,)), dma((6,)), dma((6,)), dma((4,)), dma((4,)),
            ],
            compiler_params=pltpu.CompilerParams(
                collective_id=0, has_side_effects=True, vmem_limit_bytes=44 * 1024 * 1024),
        )(keep(hidden_in), keep(w1), keep(b1.reshape(1, CH)), keep(jnp.transpose(w2, (0, 1, 3, 2))), keep(b2),
          keep(state), keep(jnp.asarray(tables)))
        return jnp.transpose(vel, (0, 2, 1, 3)), jnp.transpose(tend, (0, 2, 1, 3))

    spread = P(None, None, "lon", "lat")
    return jax.shard_map(
        body, mesh=mesh, in_specs=(spread, P(), P(), P(), P(), spread),
        out_specs=(spread, spread), check_vma=False)
```

```python
import functools
import math

import jax
import jax.numpy as jnp
import numpy as np
from jax import lax
from jax.experimental import pallas as pl
from jax.experimental.pallas import tpu as pltpu
from jax.sharding import PartitionSpec as P

MESH = pl.DeviceIdType.MESH
F32 = jnp.float32
BF16 = jnp.bfloat16
TIME_STEP = 0.5
SPEED_CAP = 0.6
COS_FLOOR = 0.5
NV = 6
NC = 12
NF = 18
LV = 8
NX = 16
NY = 128
CH = 128
M = 4
EX = NX + 2 * M
NR = NX + 2
NP = 2 * NC + NV
HALF = LV // 2


def lat_tables(n_lat_dev):
    n_lat = n_lat_dev * NY
    out = np.zeros((n_lat_dev, 2, LV, 2 * NY), np.float32)
    for d in range(n_lat_dev):
        lane = np.arange(2 * NY)
        y = np.where(lane < NY + NY // 2, lane, lane - 2 * NY) + d * NY
        phi = (y + 0.5) * (math.pi / n_lat) - 0.5 * math.pi
        inside = ((y >= 0) & (y < n_lat)).astype(np.float32)
        out[d, 0] = np.maximum(np.cos(phi), COS_FLOOR)[None]
        out[d, 1] = (SPEED_CAP * inside)[None]
    return out


def lanes(shape):
    return lax.broadcasted_iota(jnp.int32, shape, len(shape) - 1)


def roll(v, s):
    s = s % NY
    return v if s == 0 else pltpu.roll(v, s, v.ndim - 1)


def kernel(n_lon, n_lat, x_hbm, w1_hbm, b1_hbm, w2_hbm, b2_ref, st_hbm, tab_hbm,
           vel_ref, tend_ref,
           w1_ref, b1_ref, w2_ref, st_ref, tab_ref, arg_sem, xin, xt, ht, lhs1, lhs2, oh, ohe, bias, xe, xh, xs, xc, pm, pe, fm, fe, pk, pr, rowr, epk, epr,
           in_sem, x_s, x_r, row_s, row_r, cor_s, cor_r, lat_s, lat_r, lon_s, lon_r, q_s, q_r):
    lon = lax.axis_index("lon")
    lat = lax.axis_index("lat")
    left = (lax.rem(lon + n_lon - 1, n_lon), lat)
    right = (lax.rem(lon + 1, n_lon), lat)
    south = (lon, lat - 1)
    north = (lon, lat + 1)
    has_s = lat > 0
    has_n = lat < n_lat - 1

    for side, has in ((0, has_s), (1, has_n)):
        @pl.when(jnp.logical_not(has))
        def _():
            xh[side] = jnp.zeros((CH, NY), BF16)
            pr[side] = jnp.zeros((NP, LV, NY), F32)

    barrier = pltpu.get_barrier_semaphore()
    for dev in (left, right):
        pl.semaphore_signal(barrier, inc=1, device_id=dev, device_id_type=MESH)

    @pl.when(has_s)
    def _():
        pl.semaphore_signal(barrier, inc=1, device_id=south, device_id_type=MESH)

    @pl.when(has_n)
    def _():
        pl.semaphore_signal(barrier, inc=1, device_id=north, device_id_type=MESH)

    loads = [pltpu.make_async_copy(x_hbm.at[l], xin.at[l], in_sem.at[l]) for l in range(LV)]
    args = [pltpu.make_async_copy(src, dst, arg_sem.at[i]) for i, (src, dst) in enumerate(
        ((w1_hbm, w1_ref), (w2_hbm, w2_ref), (b1_hbm, b1_ref), (st_hbm, st_ref), (tab_hbm, tab_ref)))]
    for c in (*args[:3], *loads, *args[3:]):
        c.start()

    k_id = lax.broadcasted_iota(jnp.int32, (CH, 2 * NY), 0)
    lane2 = lanes((CH, 2 * NY))
    half = (k_id // 16) % 2
    target = half * NY + jnp.where(k_id < 64, 0, NY - 1)
    hit = lane2 == target

    @pl.loop(0, NX)
    def _(x):
        oh[x] = jnp.where(hit & (k_id % 16 == x), 1.0, 0.0).astype(BF16)
        want_hi = (k_id == NY - 1) & (lane2 == x)
        want_lo = (k_id == 0) & (lane2 == NY + x)
        ohe[x] = jnp.where(want_hi | want_lo, 1.0, 0.0).astype(BF16)

    for c in args[:3]:
        c.wait()
    for b in range(3):
        for a in range(3):
            lhs1[0, b * CH:(b + 1) * CH, a * CH:(a + 1) * CH] = jnp.transpose(w1_ref[a, b], (1, 0))
    for lp in range(1, LV // 2):
        lhs1[lp, :, 0:3 * CH] = lhs1[0, :, 0:3 * CH]
    lhs2[...] = jnp.zeros_like(lhs2)
    for b in range(3):
        for off in range(4):
            for r in range(2):
                a = r - off + 2
                if 0 <= a <= 2:
                    base = b * 64 + off * 16
                    lhs2[base:base + NC, r * CH:(r + 1) * CH] = w2_ref[a, b]
    bias[...] = jnp.transpose(jnp.broadcast_to(b1_ref[...], (CH, CH)), (1, 0))
    ht[:, 0] = jnp.zeros((LV, CH, NY), BF16)
    ht[:, NX + 1] = jnp.zeros((LV, CH, NY), BF16)

    def rcopy(src, dst, ss, rs_, dev):
        return pltpu.make_async_remote_copy(src_ref=src, dst_ref=dst, send_sem=ss, recv_sem=rs_,
                                            device_id=dev, device_id_type=MESH)

    hi = jnp.zeros((CH, NY), F32)
    lo = jnp.zeros((CH, NY), F32)
    rows_left, rows_right = [], []
    for l in range(LV):
        loads[l].wait()
        xt[l, 1:NX + 1] = jnp.transpose(xin[l], (1, 0, 2))
        if l % 2 == 1:
            row = jnp.concatenate(
                [jnp.concatenate([xt[l - 1 + h, 1 + x] for x in range(NX)], axis=1) for h in range(2)], axis=0)
            res = jnp.dot(row, ohe[...].reshape(NX * NY, 2 * NY), preferred_element_type=F32)
            for h in range(2):
                hi = hi + roll(res[h * CH:(h + 1) * CH, :NY], 16 * (l - 1 + h))
                lo = lo + roll(res[h * CH:(h + 1) * CH, NY:], 16 * (l - 1 + h))
        if l == HALF - 1:
            pl.semaphore_wait(barrier, 2 + has_s.astype(jnp.int32) + has_n.astype(jnp.int32))
        if (l + 1) % HALF == 0:
            g = l // HALF
            part = slice(g * HALF, (g + 1) * HALF)
            rows_left.append(rcopy(xt.at[part, 1], xt.at[part, NX + 1], row_s.at[g], row_r.at[g], left))
            rows_right.append(rcopy(xt.at[part, NX], xt.at[part, 0], row_s.at[2 + g], row_r.at[2 + g], right))
            if g == 0:
                rows_left[0].start()
                rows_right[0].start()
    xe[0] = hi.astype(BF16)
    xe[1] = lo.astype(BF16)

    def lat_exchange(src_n, src_s, dst_from_s, dst_from_n, sems, semr, at):
        to_n = rcopy(src_n, dst_from_s, sems.at[at], semr.at[at], north)
        to_s = rcopy(src_s, dst_from_n, sems.at[at + 1], semr.at[at + 1], south)

        @pl.when(has_n)
        def _():
            to_n.start()

        @pl.when(has_s)
        def _():
            to_s.start()

        def finish():
            @pl.when(has_s)
            def _():
                to_n.wait_recv()
                to_s.wait_send()

            @pl.when(has_n)
            def _():
                to_s.wait_recv()
                to_n.wait_send()
        return finish

    lane8 = lanes((LV, NY))

    def pack_lat(slot, cells):
        to_n = jnp.zeros((LV, NY), F32)
        to_s = jnp.zeros((LV, NY), F32)
        for i, (m, e) in enumerate(cells):
            mine = (lane8 >= 5 * i) & (lane8 < 5 * i + 5)
            to_n = jnp.where(mine, roll(jnp.where(lane8 == 0, e, m), 5 * i + 4), to_n)
            to_s = jnp.where(mine, roll(jnp.where(lane8 == NY - 1, e, m), 5 * i + 1), to_s)
        pk[0, slot] = to_n
        pk[1, slot] = to_s

    def send_lat(lo_, hi_, at):
        return lat_exchange(pk.at[0, lo_:hi_], pk.at[1, lo_:hi_], pr.at[0, lo_:hi_], pr.at[1, lo_:hi_],
                            lat_s, lat_r, at)

    def from_lat(slot, i):
        a = roll(pr[0, slot], -(5 * i + 4))
        b = roll(pr[1, slot], -(5 * i + 1))
        fix = jnp.where(lane8 == 0, a, jnp.where(lane8 == NY - 1, b, 0.0))
        ext = jnp.where(lane8 >= NY - 4, a, jnp.where(lane8 < 4, b, 0.0))
        return fix, ext

    def pack_rows(exts, fixes):
        acc = jnp.zeros((LV, NY), F32)
        for r in range(len(exts)):
            acc = jnp.where((lane8 >= 8 * r) & (lane8 < 8 * r + 8), roll(exts[r], 8 * r + 4), acc)
        for r in range(len(fixes)):
            acc = jnp.where((lane8 >= 40 + 2 * r) & (lane8 < 42 + 2 * r), roll(fixes[r], 41 + 2 * r), acc)
        return acc

    x_lat = lat_exchange(xe.at[0], xe.at[1], xh.at[0], xh.at[1], x_s, x_r, 0)

    zero8 = jnp.zeros((LV, NY), F32)
    for c in args[3:]:
        c.wait()
    for v in range(NV):
        fm[NC + v, M:M + NX] = jnp.transpose(st_ref[v], (1, 0, 2))

    @pl.loop(0, NV, unroll=2)
    def _(v):
        pack_lat(2 * NC + v, [(fm[NC + v, M + x], zero8) for x in range(NX)])

    x_lat()
    xpos = lanes((CH, NY)) % NX
    h0, h1 = xh[0].astype(F32), xh[1].astype(F32)
    xs[0] = jnp.where(xpos == 0, h0, roll(h1, 1)).astype(BF16)
    xs[1] = jnp.where(xpos == NX - 1, h0, roll(h1, -1)).astype(BF16)
    c_left = rcopy(xs.at[0], xc.at[1], cor_s.at[0], cor_r.at[0], left)
    c_right = rcopy(xs.at[1], xc.at[0], cor_s.at[1], cor_r.at[1], right)
    c_left.start()
    c_right.start()
    rows_left[1].start()
    rows_right[1].start()
    q_copies = [
        rcopy(fm.at[NC:NF, M:M + 4], fm.at[NC:NF, M + NX:M + NX + 4], q_s.at[0], q_r.at[0], left),
        rcopy(fm.at[NC:NF, M + NX - 4:M + NX], fm.at[NC:NF, 0:4], q_s.at[1], q_r.at[1], right)]
    for c in q_copies:
        c.start()

    def inject(corners):
        kinds = []
        for side in range(2):
            b = 2 * side
            own = xh[side].astype(F32)
            t0, t2 = roll(own, 1), roll(own, -1)
            if corners:
                t0 = jnp.where(xpos == 0, roll(xc[0].astype(F32), side - (NX - 1)), t0)
                t2 = jnp.where(xpos == NX - 1, roll(xc[1].astype(F32), NX - 1 - side), t2)
            taps = jnp.concatenate([t0.astype(BF16), xh[side], t2.astype(BF16)], axis=0)
            e = jnp.dot(lhs1[0, b * CH:(b + 1) * CH, 0:3 * CH], taps, preferred_element_type=F32)
            e_hi = e.astype(BF16).astype(F32)
            kinds += [e_hi, e - e_hi]
        group = lanes((CH, NY)) // 32
        for lp in range(LV // 2):
            inj = jnp.zeros((CH, NY), F32)
            for kind in range(4):
                inj = jnp.where(group == kind, roll(kinds[kind], 32 * kind - 32 * lp), inj)
            lhs1[lp, CH:2 * CH, 3 * CH:] = inj.astype(BF16)
            if not corners:
                lhs1[lp, 0:CH, 3 * CH:] = jnp.zeros((CH, NY), BF16)
                lhs1[lp, 2 * CH:, 3 * CH:] = jnp.zeros((CH, NY), BF16)

    inject(False)

    q_lat = send_lat(2 * NC, NP, 4)

    lane1 = lanes((CH, NY))

    def conv1(lp, x):
        rhs = jnp.concatenate(
            [xt[2 * lp + h, pl.ds(x, 3)].reshape(3 * CH, NY) for h in range(2)], axis=1)
        rhs = jnp.concatenate([rhs, oh[x]], axis=0)
        s = jnp.dot(lhs1[lp], rhs, preferred_element_type=F32)
        for h in range(2):
            c = slice(h * NY, (h + 1) * NY)
            pre = s[CH:2 * CH, c] + bias[...]
            pre = pre + jnp.where(lane1 == 0, 0.0, roll(s[0:CH, c], 1))
            pre = pre + jnp.where(lane1 == NY - 1, 0.0, roll(s[2 * CH:, c], -1))
            half_pre = 0.5 * pre
            ht[2 * lp + h, x + 1] = (half_pre + half_pre * jnp.tanh(half_pre)).astype(BF16)

    lane64 = lanes((64, NY))

    def conv2(lp, j):
        rhs = jnp.concatenate(
            [ht[2 * lp + h, 2 * j:2 * j + 2].reshape(2 * CH, NY) for h in range(2)], axis=1)
        s = jnp.dot(lhs2[...], rhs, preferred_element_type=F32)
        out = []
        for h in range(2):
            c = slice(h * NY, (h + 1) * NY)
            up = roll(s[0:64, c], 1)
            dn = roll(s[128:192, c], -1)
            main = s[64:128, c] + jnp.where(lane64 == 0, 0.0, up) + jnp.where(lane64 == NY - 1, 0.0, dn)
            edge = jnp.where(lane64 == 0, up, 0.0) + jnp.where(lane64 == NY - 1, dn, 0.0)
            out.append((main, edge))
        return out

    def put(lp, row, parts, more=False):
        for h in range(2):
            at = pl.ds(row * (NC * LV) + 2 * lp + h, NC, stride=LV)
            for k, ref in enumerate((pm, pe)):
                t = None
                for pair, off in parts:
                    piece = pair[h][k][off * 16:off * 16 + NC]
                    t = piece if t is None else t + piece
                ref[at, :] = ref[at, :] + t if more else t

    def cell(row, f):
        at = pl.ds(pl.multiple_of((row * NC + f) * LV, LV), LV)
        return pm[at, :], pe[at, :]

    @pl.loop(0, LV)
    def _(i):
        lp, g = i // 2, i % 2
        for u in range(4):
            conv1(lp, 1 + 10 * g + u)

    for c in (c_left, c_right, *rows_left, *rows_right):
        c.wait()
    inject(True)

    @pl.loop(0, LV // 4)
    def _(i):
        for u in range(2):
            conv1(2 * i + u, 0)
            conv1(2 * i + u, NX - 1)

    q_lat()

    @pl.loop(0, NV, unroll=2)
    def _(v):
        exts = []
        for x in range(NX):
            _, ext = from_lat(2 * NC + v, x)
            fe[NC + v, M + x] = ext
            exts.append(ext)
        epk[0, NC + v] = pack_rows(exts[:4], [])
        epk[1, NC + v] = pack_rows(exts[-4:], [])

    q_edges = [
        rcopy(epk.at[0, NC:NF], epr.at[1, NC:NF], q_s.at[2], q_r.at[2], left),
        rcopy(epk.at[1, NC:NF], epr.at[0, NC:NF], q_s.at[3], q_r.at[3], right)]
    for c in q_edges:
        c.start()

    @pl.loop(0, LV // 2)
    def _(lp):
        p = [conv2(lp, j) for j in range(3)]
        put(lp, 0, [(p[0], 1)])
        for i in range(2):
            put(lp, 1 + i, [(p[0], 2 + i), (p[1], i)])
            put(lp, 3 + i, [(p[1], 2 + i), (p[2], i)])
            put(lp, 5 + i, [(p[2], 2 + i)])
        p = [conv2(lp, j) for j in range(6, 9)]
        for i in range(2):
            put(lp, 11 + i, [(p[0], i)])
            put(lp, 13 + i, [(p[0], 2 + i), (p[1], i)])
            put(lp, 15 + i, [(p[1], 2 + i), (p[2], i)])
        put(lp, 17, [(p[2], 2)])

    def rows_part(k, lo_, hi_):
        at, to = pl.ds(lo_ * NC * LV, (hi_ - lo_) * NC * LV), NR - 5
        far = pl.ds((to + lo_) * NC * LV, (hi_ - lo_) * NC * LV)
        return [rcopy(pm.at[at], rowr.at[1, at], lon_s.at[k], lon_r.at[k], left),
                rcopy(pm.at[far], rowr.at[0, at], lon_s.at[k + 1], lon_r.at[k + 1], right)]

    first_rows = rows_part(0, 0, 2)
    last_rows = rows_part(4, 2, 5)
    for c in first_rows:
        c.start()

    outer = [0, 1, 2, 3, 4, NR - 5, NR - 4, NR - 3, NR - 2, NR - 1]
    inner = list(range(5, NR - 5))

    @pl.loop(0, NC, unroll=2)
    def _(f):
        pack_lat(f, [cell(r, f) for r in outer])

    outer_lat = send_lat(0, NC, 0)

    @pl.loop(0, LV // 2)
    def _(lp):
        for x in range(5, NX - 7):
            conv1(lp, x)

    outer_lat()
    for c in last_rows:
        c.start()

    @pl.loop(0, LV // 4)
    def _(i):
        for u in range(2):
            for x in range(NX - 7, NX - 5):
                conv1(2 * i + u, x)

    def take(slot, i, row, f):
        m, e = cell(row, f)
        fix, ext = from_lat(slot, i)
        fm[f, M - 1 + row] = m + fix
        fe[f, M - 1 + row] = e + ext
        return fix, e + ext

    @pl.loop(0, NC, unroll=2)
    def _(f):
        got = [take(f, i, r, f) for i, r in enumerate(outer)]
        epk[0, f] = pack_rows([g[1] for g in got[:5]], [g[0] for g in got[:5]])
        epk[1, f] = pack_rows([g[1] for g in got[5:]], [g[0] for g in got[5:]])

    e_left = rcopy(epk.at[0, 0:NC], epr.at[1, 0:NC], lon_s.at[2], lon_r.at[2], left)
    e_right = rcopy(epk.at[1, 0:NC], epr.at[0, 0:NC], lon_s.at[3], lon_r.at[3], right)
    e_left.start()
    e_right.start()

    @pl.loop(0, LV // 2)
    def _(lp):
        p = [conv2(lp, j) for j in range(3, 6)]
        for i in range(2):
            put(lp, 5 + i, [(p[0], i)], True)
            put(lp, 7 + i, [(p[0], 2 + i), (p[1], i)])
            put(lp, 9 + i, [(p[1], 2 + i), (p[2], i)])
            put(lp, 11 + i, [(p[2], 2 + i)], True)

    @pl.loop(0, NC, unroll=2)
    def _(f):
        pack_lat(NC + f, [cell(r, f) for r in inner])

    inner_lat = send_lat(NC, 2 * NC, 2)

    for c in (*q_copies, *q_edges):
        c.wait()

    def ext_lanes(t):
        return jnp.where((lane8 < 4) | (lane8 >= NY - 4), t, 0.0)

    @pl.loop(NC, NF)
    def _(f):
        for side in range(2):
            t = epr[side, f]
            for r in range(4):
                fe[f, (0 if side == 0 else M + NX) + r] = ext_lanes(roll(t, -(8 * r + 4)))

    inner_lat()

    @pl.loop(0, NC, unroll=2)
    def _(f):
        for i, r in enumerate(inner):
            take(NC + f, i, r, f)

    for c in (*first_rows, *last_rows, e_left, e_right):
        c.wait()

    @pl.loop(0, NC, unroll=2)
    def _(f):
        for side in range(2):
            t = epr[side, f]
            for r in range(5):
                x = (r if side == 0 else M + NX - 1 + r)
                fix = jnp.where((lane8 == 0) | (lane8 == NY - 1), roll(t, -(41 + 2 * r)), 0.0)
                got = rowr[side, pl.ds(pl.multiple_of((r * NC + f) * LV, LV), LV), :] + fix
                ext = ext_lanes(roll(t, -(8 * r + 4)))
                if x < M - 1 or x > M + NX:
                    fm[f, x] = got
                    fe[f, x] = ext
                else:
                    fm[f, x] = fm[f, x] + got
                    fe[f, x] = fe[f, x] + ext

    cos_m = tab_ref[lat, 0, :, 0:NY]
    cos_e = tab_ref[lat, 0, :, NY:]
    cap_m = tab_ref[lat, 1, :, 0:NY]
    cap_e = tab_ref[lat, 1, :, NY:]
    met_m = 1.0 / cos_m
    met_e = 1.0 / cos_e

    def shift(m, e, step):
        sh = 1 if step < 0 else -1
        edge = 0 if step < 0 else NY - 1
        rm, re = roll(m, sh), roll(e, sh)
        at = lanes(m.shape) == edge
        return jnp.where(at, re, rm), jnp.where(at, rm, re)

    @pl.loop(0, NV)
    def _(v):
        bu = b2_ref[2 * v]
        bv = b2_ref[2 * v + 1]
        um = cap_m * jnp.tanh(fm[2 * v] + bu)
        ue = cap_e * jnp.tanh(fe[2 * v] + bu)
        vm = cap_m * jnp.tanh(fm[2 * v + 1] + bv)
        ve = cap_e * jnp.tanh(fe[2 * v + 1] + bv)
        vel_ref[2 * v] = um[M:M + NX]
        vel_ref[2 * v + 1] = vm[M:M + NX]
        i = slice(1, EX - 1)
        fn_m, fn_e = shift(vm[i] * cos_m, ve[i] * cos_e, 1)
        fs_m, fs_e = shift(vm[i] * cos_m, ve[i] * cos_e, -1)

        def coef(u, vv, met, fn, fs):
            div = met * ((u[2:] - u[:-2]) * 0.5 + (fn - fs) * 0.5)
            up, un = met * jnp.maximum(u[i], 0.0), met * jnp.minimum(u[i], 0.0)
            vp, vn = jnp.maximum(vv[i], 0.0), jnp.minimum(vv[i], 0.0)
            return (un - up) + (vn - vp) - div, up, un, vp, vn

        cm = coef(um, vm, met_m, fn_m, fs_m)
        ce = coef(ue, ve, met_e, fn_e, fs_e)

        def rate(qm, qe, k):
            n = EX - 2 * k
            nm, ne = shift(qm[1:-1], qe[1:-1], 1)
            sm, se = shift(qm[1:-1], qe[1:-1], -1)

            def one(q, c, qn, qs):
                c0, up, un, vp, vn = (t[k - 1:k - 1 + n] for t in c)
                return c0 * q[1:-1] + up * q[:-2] - un * q[2:] + vp * qs - vn * qn
            return one(qm, cm, nm, sm), one(qe, ce, ne, se)

        qm = fm[NC + v]
        qe = fe[NC + v]
        r1m, r1e = rate(qm, qe, 1)
        tot = r1m[3:3 + NX]
        r2m, r2e = rate(qm[1:-1] + 0.25 * r1m, qe[1:-1] + 0.25 * r1e, 2)
        tot = tot + 2.0 * r2m[2:2 + NX]
        r3m, r3e = rate(qm[2:-2] + 0.25 * r2m, qe[2:-2] + 0.25 * r2e, 3)
        tot = tot + 2.0 * r3m[1:1 + NX]
        r4m, _ = rate(qm[3:-3] + 0.5 * r3m, qe[3:-3] + 0.5 * r3e, 4)
        tend_ref[v] = (tot + r4m) * (1.0 / 6.0)


def solution(mesh):
    n_lon, n_lat = mesh.shape["lon"], mesh.shape["lat"]
    tables = lat_tables(n_lat)

    def body(hidden_in, w1, b1, w2, b2, state):
        vmem = pl.BlockSpec(memory_space=pltpu.VMEM)
        hbm = pl.BlockSpec(memory_space=pltpu.HBM)

        def keep(array):
            return pltpu.with_memory_space_constraint(array, pltpu.HBM)
        dma = pltpu.SemaphoreType.DMA
        vel, tend = pl.pallas_call(
            functools.partial(kernel, n_lon, n_lat),
            out_shape=(jax.ShapeDtypeStruct((NC, NX, LV, NY), F32),
                       jax.ShapeDtypeStruct((NV, NX, LV, NY), F32)),
            in_specs=[hbm, hbm, hbm, hbm, pl.BlockSpec(memory_space=pltpu.SMEM), hbm, hbm],
            out_specs=(vmem, vmem),
            scratch_shapes=[
                pltpu.VMEM(w1.shape, BF16),
                pltpu.VMEM((1, CH), F32),
                pltpu.VMEM((3, 3, NC, CH), BF16),
                pltpu.VMEM((NV, LV, NX, NY), F32),
                pltpu.VMEM(tables.shape, F32),
                dma((5,)),
                pltpu.VMEM((LV, CH, NX, NY), BF16),
                pltpu.VMEM((LV, NX + 2, CH, NY), BF16),
                pltpu.VMEM((LV, NX + 2, CH, NY), BF16),
                pltpu.VMEM((LV // 2, 3 * CH, 4 * CH), BF16),
                pltpu.VMEM((192, 2 * CH), BF16),
                pltpu.VMEM((NX, CH, 2 * NY), BF16),
                pltpu.VMEM((NX, CH, 2 * NY), BF16),
                pltpu.VMEM((CH, NY), F32),
                pltpu.VMEM((2, CH, NY), BF16),
                pltpu.VMEM((2, CH, NY), BF16),
                pltpu.VMEM((2, CH, NY), BF16),
                pltpu.VMEM((2, CH, NY), BF16),
                pltpu.VMEM((NR * NC * LV + 8 * LV, NY), F32),
                pltpu.VMEM((NR * NC * LV + 8 * LV, NY), F32),
                pltpu.VMEM((NF, EX, LV, NY), F32),
                pltpu.VMEM((NF, EX, LV, NY), F32),
                pltpu.VMEM((2, NP, LV, NY), F32),
                pltpu.VMEM((2, NP, LV, NY), F32),
                pltpu.VMEM((2, 5 * NC * LV, NY), F32),
                pltpu.VMEM((2, NF, LV, NY), F32),
                pltpu.VMEM((2, NF, LV, NY), F32),
                dma((LV,)), dma((2,)), dma((2,)), dma((4,)), dma((4,)), dma((2,)), dma((2,)),
                dma((6,)), dma((6,)), dma((6,)), dma((6,)), dma((4,)), dma((4,)),
            ],
            compiler_params=pltpu.CompilerParams(
                collective_id=0, has_side_effects=True, vmem_limit_bytes=44 * 1024 * 1024),
        )(keep(hidden_in), keep(w1), keep(b1.reshape(1, CH)), keep(jnp.transpose(w2, (0, 1, 3, 2))), keep(b2),
          keep(state), keep(jnp.asarray(tables)))
        return jnp.transpose(vel, (0, 2, 1, 3)), jnp.transpose(tend, (0, 2, 1, 3))

    spread = P(None, None, "lon", "lat")
    return jax.shard_map(
        body, mesh=mesh, in_specs=(spread, P(), P(), P(), P(), spread),
        out_specs=(spread, spread), check_vma=False)
```
